32 devices in a mesh: grp: 2 (over x), seq: 16 (over z, y, core).
Axes of the slice: x: 2, y: 2, z: 4, core: 2. Of those that a mesh axis runs over, the one named last changes fastest.
Arguments:
- fast_state: bfloat16 [32, 3, 1024, 512], P(('grp', 'seq')), parts along dimension 0, may hold values from -0.25 to 0.25
- initial_fast: bfloat16 [3, 1024, 512], P(None, 'seq'), may hold values from -0.25 to 0.25
- queries: bfloat16 [32, 4, 384, 512], P(('grp', 'seq')), parts along dimension 0, may hold values from -6 to 6
- token_keys: bfloat16 [32, 4, 384, 512], P(('grp', 'seq')), parts along dimension 0, may hold values from -6 to 6
- token_values: bfloat16 [32, 4, 384, 512], P(('grp', 'seq')), parts along dimension 0, may hold values from -6 to 6
- step_sizes: bfloat16 [32, 4, 384], P(('grp', 'seq')), parts along dimension 0, may hold values from 0.0019989014 to 0.019897461
Outputs:
- layer_output: bfloat16 [32, 4, 384, 512], P(('grp', 'seq')), parts along dimension 0
The draws below stay inside these ranges and needn't reach their ends.
There are 2 independent parts, one for each index of `grp`. The reference program is written for one: setup_inputs(seed, part) draws one part's arguments, and reference() takes and returns one part's arrays. A program takes and returns all parts, laid end to end along the dimension named above; an argument that names none is the same for every part. Nothing has to cross between parts.
All inputs are finite; a program needn't handle non-finite values.
Results may differ from the reference program's by a relative error of at most 0.012.
The reference program's roundings to bfloat16 on the way count: a program that leaves them out, or rounds other values in their place, can miss the bound.
Values may be sent and summed in bfloat16 or wider, within the bound.
No kernel may reach another device: no remote copies, remote signals or barrier semaphores. Data moves between devices by JAX's collectives and lax.ppermute only.
A program may use at most 64 MiB of HBM per device.

```python
import math
import jax
import jax.numpy as jnp
from jax import lax

DK = 512
HID = 1024
SPAN = 384
TICKS = 4
SECTIONS = 16


def shard_levels(own_key, extent, shards, least, high):
    factor_of = 1.0
    for position, blocks in shards:
        heights = jax.random.uniform(jax.random.fold_in(jax.random.fold_in(own_key, 6), position), (blocks,), jnp.float32, least / len(shards), high / len(shards))
        factor_of = factor_of * jnp.repeat(jnp.exp(heights), extent[position] // blocks).reshape((-1,) + (1,) * (len(extent) - 1 - position))
    return factor_of


def bell_draw(key, dims, width, most, cuts=(), dtype=jnp.bfloat16):
    array = jax.random.normal(key, dims, jnp.float32) * width
    if len(cuts) > 0:
        array = shard_levels(key, dims, cuts, -0.22, 0.18) * array
    return jnp.clip(array, min=-most, max=most).astype(dtype)


def setup_inputs(seed: int = 0, part: int = 0) -> dict:
    seeds = jax.random.split(jax.random.key(seed), 7)
    own_keys = jax.random.split(jax.random.fold_in(seeds[6], part), 7)
    return {
        "fast_state": bell_draw(own_keys[0], (SECTIONS, 3, HID, DK), DK ** -0.5, 0.25, ((0, 16),)),
        "initial_fast": bell_draw(seeds[1], (3, HID, DK), DK ** -0.5, 0.25, ((1, 16),)),
        "queries": bell_draw(own_keys[2], (SECTIONS, TICKS, SPAN, DK), 1.0, 6.0, ((0, 16),)),
        "token_keys": bell_draw(own_keys[3], (SECTIONS, TICKS, SPAN, DK), 1.0, 6.0, ((0, 16),)),
        "token_values": bell_draw(own_keys[4], (SECTIONS, TICKS, SPAN, DK), 1.0, 6.0, ((0, 16),)),
        "step_sizes": jnp.clip(jnp.exp(math.log(0.019897461) - 2.2979944 * jax.random.uniform(own_keys[5], (SECTIONS, TICKS, SPAN), jnp.float32) ** shard_levels(own_keys[5], (SECTIONS, TICKS, SPAN), ((0, 16),), -0.2, 0.2)), 0.0019989014, 0.019897461).astype(jnp.bfloat16),
    }


epsilon = 1e-06

def contract_last(left_side, right_side):
    return lax.dot_general(left_side, right_side, (((1,), (1,)), ((), ())), preferred_element_type=jnp.float32)

def contract_first(left_side, right_side):
    return lax.dot_general(left_side, right_side, (((0,), (0,)), ((), ())), preferred_element_type=jnp.float32)

def rescale(updated, previous):
    old_norm = jnp.sqrt(lax.optimization_barrier(jnp.sum(previous * previous, axis=-1, keepdims=True)) + epsilon)
    new_norm = jnp.sqrt(lax.optimization_barrier(jnp.sum(updated * updated, axis=-1, keepdims=True)) + epsilon)
    return updated * (old_norm / new_norm)

def advance(fast, token_keys, token_values, step_sizes):
    gate_pre = contract_last(token_keys, fast[0])
    up_pre = contract_last(token_keys, fast[1])
    gate_sig = jax.nn.sigmoid(gate_pre)
    hidden = (gate_pre * gate_sig * up_pre).astype(jnp.bfloat16)
    target = (step_sizes.astype(jnp.float32)[:, None] * token_values.astype(jnp.float32)).astype(jnp.bfloat16)
    back_grad = contract_last(target, fast[2])
    grad_gate = (back_grad * up_pre * gate_sig * (1.0 + gate_pre * (1.0 - gate_sig))).astype(jnp.bfloat16)
    grad_up = (back_grad * gate_pre * gate_sig).astype(jnp.bfloat16)
    delta_gate = contract_first(grad_gate, token_keys)
    delta_up = contract_first(grad_up, token_keys)
    delta_down = contract_first(hidden, target)
    previous = fast.astype(jnp.float32)
    updated = previous + jnp.stack([delta_gate, delta_up, delta_down])
    return rescale(updated, previous).astype(jnp.bfloat16)

def serve_queries(fast, queries):
    gate_pre = contract_last(queries, fast[0])
    up_pre = contract_last(queries, fast[1])
    hidden = (gate_pre * jax.nn.sigmoid(gate_pre) * up_pre).astype(jnp.bfloat16)
    return jnp.dot(hidden, fast[2], preferred_element_type=jnp.float32).astype(jnp.bfloat16)

def reference(fast_state, initial_fast, queries, token_keys, token_values, step_sizes):
    carried = fast_state
    results = []
    advanced = fast_state
    for step_index in range(TICKS):
        if step_index > 0:
            carried = jnp.concatenate([initial_fast[None], advanced[:-1]], axis=0)
        advanced = lax.map(lambda section_item: advance(*section_item), (carried, token_keys[:, step_index], token_values[:, step_index], step_sizes[:, step_index]))
        served = lax.map(lambda section_item: serve_queries(*section_item), (advanced, queries[:, step_index]))
        results.append(served)
    return jnp.stack(results, axis=1)
```

```python
import functools
import jax
import jax.numpy as jnp
from jax import lax
from jax.experimental import pallas as pl
from jax.experimental.pallas import tpu as pltpu
from jax.sharding import PartitionSpec as P

epsilon = 1e-06
f32 = jnp.float32
bf16 = jnp.bfloat16


def nt(a, b):
    return lax.dot_general(a, b, (((1,), (1,)), ((), ())), preferred_element_type=f32)


def tn(a, b):
    return lax.dot_general(a, b, (((0,), (0,)), ((), ())), preferred_element_type=f32)


def nn(a, b):
    return lax.dot_general(a, b, (((1,), (0,)), ((), ())), preferred_element_type=f32)


def scaled_values(steps_row, values):
    lanes = 128
    span, width = values.shape
    column = jnp.broadcast_to(steps_row.astype(f32), (lanes, span)).T
    return jnp.concatenate(
        [
            (column * values[:, i : i + lanes].astype(f32)).astype(bf16)
            for i in range(0, width, lanes)
        ],
        axis=1,
    )


def pack_kernel(tick, k_ref, v_ref, q_ref, r_ref, o_ref):
    o_ref[0] = k_ref[...]
    o_ref[1] = scaled_values(r_ref[tick : tick + 1, :], v_ref[...])
    o_ref[2] = q_ref[...]


def pack(tick, keys, values, queries, steps):
    _, ticks, span, width = keys.shape
    one = pl.BlockSpec((None, None, span, width), lambda i: (0, tick, 0, 0))
    return pl.pallas_call(
        functools.partial(pack_kernel, tick),
        grid=(1,),
        in_specs=[one, one, one, pl.BlockSpec((None, ticks, span), lambda i: (0, 0, 0))],
        out_specs=pl.BlockSpec((3, span, width), lambda i: (0, 0, 0)),
        out_shape=jax.ShapeDtypeStruct((3, span, width), bf16),
        name=f"pack{tick}",
    )(keys, values, queries, steps)


def step_rows(old, delta):
    previous = old.astype(f32)
    updated = previous + delta
    old_norm = jnp.sqrt(jnp.sum(previous * previous, axis=-1, keepdims=True) + epsilon)
    new_norm = jnp.sqrt(jnp.sum(updated * updated, axis=-1, keepdims=True) + epsilon)
    return (updated * (old_norm / new_norm)).astype(bf16)


def unit_block(keys, target, queries, gate, up, down):
    gate_pre = nt(keys, gate)
    up_pre = nt(keys, up)
    back_grad = nt(target, down)
    sig = jax.nn.sigmoid(gate_pre)
    silu = gate_pre * sig
    hidden = (silu * up_pre).astype(bf16)
    grad_up = (back_grad * silu).astype(bf16)
    grad_gate = (back_grad * up_pre * sig * (1.0 + gate_pre * (1.0 - sig))).astype(bf16)
    new_gate = step_rows(gate, tn(grad_gate, keys))
    new_up = step_rows(up, tn(grad_up, keys))
    new_down = step_rows(down, tn(hidden, target))
    c = nt(queries, new_gate)
    e = nt(queries, new_up)
    served = (c * jax.nn.sigmoid(c) * e).astype(bf16)
    return new_gate, new_up, new_down, nn(served, new_down)


def unit_kernel(raw, two_tokens, two_states, flags_ref, *refs):
    refs = list(refs)
    take = lambda n: [refs.pop(0) for _ in range(n)]
    if raw:
        k_ref, v_ref, q_ref, r_ref = take(4)
    else:
        packs = take(2 if two_tokens else 1)
    states = take(2 if two_states else 1)
    take(1)
    new_ref, ans_ref, tokens, acc = refs
    step = pl.program_id(0)

    @pl.when(flags_ref[0] != 0)
    def _():
        @pl.when(step == 0)
        def _():
            if raw:
                tokens[0] = k_ref[...]
                tokens[1] = scaled_values(r_ref[0:1, :], v_ref[...])
                tokens[2] = q_ref[...]
            elif two_tokens:
                @pl.when(flags_ref[1] != 0)
                def _():
                    tokens[...] = packs[1][...]

                @pl.when(flags_ref[1] == 0)
                def _():
                    tokens[...] = packs[0][...]

            acc[...] = jnp.zeros_like(acc)

        source = tokens if (raw or two_tokens) else packs[0]
        old = [states[0][i] for i in range(3)]
        if two_states:
            pick = flags_ref[2] != 0
            old = [jnp.where(pick, states[1][i], old[i]) for i in range(3)]
        new_gate, new_up, new_down, part = unit_block(
            source[0], source[1], source[2], *old
        )
        new_ref[0] = new_gate
        new_ref[1] = new_up
        new_ref[2] = new_down
        acc[...] += part

        @pl.when(step == pl.num_programs(0) - 1)
        def _():
            ans_ref[...] = acc[...].astype(bf16)


def unit(name, flags, tokens, states, after, raw=False, ticks=None, block=256):
    width = tokens[0].shape[-1]
    span = tokens[0].shape[-2]
    hid = states[0].shape[-2]
    lead = (None,) * (states[0].ndim - 3)
    zeros = (0,) * (states[0].ndim - 3)
    two_tokens = (not raw) and len(tokens) == 2
    two_states = len(states) == 2
    if raw:
        first = pl.BlockSpec((None, None, span, width), lambda i, f: (0, 0, 0, 0))
        token_specs = [first] * 3 + [
            pl.BlockSpec((None,) + tokens[3].shape[1:], lambda i, f: (0, 0, 0))
        ]
        ans_spec = pl.BlockSpec((None, None, span, width), lambda i, f: (0, 0, 0, 0))
        ans_shape = tokens[0].shape
    else:
        token_specs = [
            pl.BlockSpec((3, span, width), lambda i, f: (0, 0, 0)) for _ in tokens
        ]
        ans_spec = pl.BlockSpec((span, width), lambda i, f: (0, 0))
        ans_shape = (span, width)

    def state_map(second):
        def index(i, f):
            use = f[0] if not two_states else f[0] * (f[2] if second else 1 - f[2])
            return zeros + (0, i * use, 0)
        return index

    state_specs = [
        pl.BlockSpec(lead + (3, block, width), state_map(n == 1))
        for n in range(len(states))
    ]
    return pl.pallas_call(
        functools.partial(unit_kernel, raw, two_tokens, two_states),
        grid_spec=pltpu.PrefetchScalarGridSpec(
            num_scalar_prefetch=1,
            grid=(hid // block,),
            in_specs=token_specs + state_specs + [pl.BlockSpec(memory_space=pl.ANY)],
            out_specs=[
                pl.BlockSpec((3, block, width), lambda i, f: (0, i * f[0], 0)),
                ans_spec,
            ],
            scratch_shapes=[
                pltpu.VMEM((3, span, width) if (raw or two_tokens) else (8, 128), bf16),
                pltpu.VMEM((span, width), f32),
            ],
        ),
        out_shape=[
            jax.ShapeDtypeStruct((3, hid, width), bf16),
            jax.ShapeDtypeStruct(ans_shape, bf16),
        ],
        name=name,
    )(flags, *tokens, *states, after)


def gather_initial(initial, position, count):
    core = 2
    held = initial
    reach = core
    while reach < count:
        pairs = []
        for start in range(0, count, 2 * reach):
            for c in range(core):
                if start + reach + c < count:
                    pairs.append((start + reach + c, start + c))
        held = jnp.concatenate([held, lax.ppermute(held, "seq", pairs)], axis=1)
        reach *= 2
    other = lax.ppermute(held, "seq", [(0, 1), (1, 0)])
    return jnp.concatenate([held, other], axis=1)


def body(fast_state, initial_fast, queries, token_keys, token_values, step_sizes):
    count = lax.axis_size("seq")
    position = lax.axis_index("seq")
    i32 = jnp.int32
    on = jnp.ones((), i32)
    off = jnp.zeros((), i32)
    flags = jnp.stack([on, off, off])
    first = (position == 0).astype(i32)
    second = (position == 1).astype(i32)
    extra = first + second
    flags_e = jnp.stack([extra, second, second])

    def send(value, pairs):
        return lax.ppermute(value, "seq", pairs)

    packs = [None] + [
        pack(t, token_keys, token_values, queries, step_sizes) for t in (1, 2, 3)
    ]
    down = lambda t: [(s, s - t) for s in range(t, count)]
    up = lambda t: [(s, s + t) for s in range(count - t)]
    tokens = [None] + [send(packs[t], down(t)) for t in (1, 2, 3)]
    cross2 = send(packs[2], [(1, 0), (0, 1)])
    cross3 = send(packs[3], [(2, 0), (0, 1)])
    whole = gather_initial(initial_fast, position, count)

    state, out = unit(
        "u0", flags, [token_keys, token_values, queries, step_sizes], [fast_state],
        step_sizes, raw=True,
    )
    s1, a1 = unit("u1", flags, [tokens[1]], [state], out)
    b1 = send(a1, up(1))
    e1, x1 = unit("e1", flags_e, [packs[1], cross2], [whole], a1)
    s2, a2 = unit("u2", flags, [tokens[2]], [s1], x1)
    b2 = send(a2, up(2))
    e2, x2 = unit("e2", flags_e, [cross2, packs[3]], [e1], a2)
    c2 = send(jnp.where(first != 0, x2, x1), [(0, 1), (1, 0)])
    e3, x3 = unit("e3", flags_e, [cross3], [e2, whole], x2)
    c3 = send(x3, [(0, 2), (1, 0)])
    s3, a3 = unit("u3", flags, [tokens[3]], [s2], x3)
    b3 = send(a3, up(3))

    r1 = jnp.where(first != 0, x1, b1)
    r2 = jnp.where(extra != 0, c2, b2)
    early3 = jnp.where(second != 0, x2, c3)
    r3 = jnp.where(position < 3, early3, b3)
    for t, r in ((1, r1), (2, r2), (3, r3)):
        out = lax.dynamic_update_slice(out, r[None, None], (0, t, 0, 0))
    return out


def solution(mesh):
    return jax.shard_map(
        body,
        mesh=mesh,
        in_specs=(
            P(("grp", "seq"), None, None, None),
            P(None, "seq", None),
            P(("grp", "seq"), None, None, None),
            P(("grp", "seq"), None, None, None),
            P(("grp", "seq"), None, None, None),
            P(("grp", "seq"), None, None),
        ),
        out_specs=P(("grp", "seq"), None, None, None),
        check_vma=False,
    )
```

```python
import functools
import jax
import jax.numpy as jnp
from jax import lax
from jax.experimental import pallas as pl
from jax.experimental.pallas import tpu as pltpu
from jax.sharding import PartitionSpec as P

epsilon = 1e-06
f32 = jnp.float32
bf16 = jnp.bfloat16
HBM = pl.BlockSpec(memory_space=pltpu.HBM)
VMEM = pl.BlockSpec(memory_space=pltpu.VMEM)
SMEM = pl.BlockSpec(memory_space=pltpu.SMEM)
LIMIT = 28 << 20


def in_hbm(*arrays):
    return [pltpu.with_memory_space_constraint(a, pltpu.HBM) for a in arrays]


def nt(a, b):
    return lax.dot_general(a, b, (((1,), (1,)), ((), ())), preferred_element_type=f32)


def nn(a, b):
    return lax.dot_general(a, b, (((1,), (0,)), ((), ())), preferred_element_type=f32)


def sigmoid(x):
    return 0.5 * jnp.tanh(0.5 * x) + 0.5


def scaled_values(steps_row, values):
    lanes = 128
    span, width = values.shape
    column = jnp.broadcast_to(steps_row.astype(f32), (lanes, span)).T
    return jnp.concatenate(
        [
            (column * values[:, i : i + lanes].astype(f32)).astype(bf16)
            for i in range(0, width, lanes)
        ],
        axis=1,
    )


def pack_kernel(tick, k_ref, v_ref, q_ref, r_ref, o_ref, vals, sems):
    copies = [
        pltpu.make_async_copy(v_ref.at[0, tick], vals, sems.at[0]),
        pltpu.make_async_copy(k_ref.at[0, tick], o_ref.at[0], sems.at[1]),
        pltpu.make_async_copy(q_ref.at[0, tick], o_ref.at[2], sems.at[2]),
    ]
    for copy in copies:
        copy.start()
    copies[0].wait()
    vals[...] = scaled_values(r_ref[0, tick : tick + 1, :], vals[...])
    back = pltpu.make_async_copy(vals, o_ref.at[1], sems.at[3])
    back.start()
    copies[1].wait()
    copies[2].wait()
    back.wait()


def pack(tick, keys, values, queries, steps):
    _, _, span, width = keys.shape
    return pl.pallas_call(
        functools.partial(pack_kernel, tick),
        in_specs=[HBM, HBM, HBM, VMEM],
        out_specs=HBM,
        out_shape=jax.ShapeDtypeStruct((3, span, width), bf16),
        scratch_shapes=[pltpu.VMEM((span, width), bf16), pltpu.SemaphoreType.DMA((4,))],
        compiler_params=pltpu.CompilerParams(vmem_limit_bytes=LIMIT),
    )(*in_hbm(keys, values, queries), steps)


def step_rows(old, delta):
    previous = old.astype(f32)
    updated = previous + delta
    old_norm = jnp.sqrt(jnp.sum(previous * previous, axis=-1, keepdims=True) + epsilon)
    new_norm = jnp.sqrt(jnp.sum(updated * updated, axis=-1, keepdims=True) + epsilon)
    return (updated * (old_norm / new_norm)).astype(bf16)


def advance_rows(keys, target, gate, up, down):
    gate_pre = nt(gate, keys)
    up_pre = nt(up, keys)
    back_grad = nt(down, target)
    sig = sigmoid(gate_pre)
    silu = gate_pre * sig
    hidden = (silu * up_pre).astype(bf16)
    grad_up = (back_grad * silu).astype(bf16)
    grad_gate = ((back_grad * up_pre) * (sig * (1.0 + (gate_pre - silu)))).astype(bf16)
    return (
        step_rows(gate, nn(grad_gate, keys)),
        step_rows(up, nn(grad_up, keys)),
        step_rows(down, nn(hidden, target)),
    )


def serve_rows(queries, gate, up, down):
    c = nt(queries, gate)
    e = nt(queries, up)
    return nn((c * sigmoid(c) * e).astype(bf16), down)


def compute(tok, old, new_ref, acc, ans, block, wait_queries):
    count = new_ref.shape[1] // block

    @pl.loop(0, count)
    def _(j):
        rows = pl.ds(pl.multiple_of(j * block, block), block)
        new = advance_rows(tok[0], tok[1], old[0, rows], old[1, rows], old[2, rows])
        for i in range(3):
            new_ref[i, rows] = new[i]

        @pl.when(j == 0)
        def _():
            wait_queries()
            acc[...] = jnp.zeros_like(acc)

        acc[...] += serve_rows(
            tok[2], new_ref[0, rows], new_ref[1, rows], new_ref[2, rows]
        )

    ans[...] = acc[...].astype(bf16)


def unit_kernel(kind, n_tokens, n_states, n_pieces, n_carry, block, flags_ref, *refs):
    refs = list(refs)
    take = lambda n: [refs.pop(0) for _ in range(n)]
    tokens = take(4 if kind == "raw" else n_tokens)
    states = take(n_states)
    pieces = take(n_pieces)
    take(n_carry)
    new_ref, ans_out = take(2)
    take(n_carry)
    tok, acc, ans, sems = take(4)
    if kind == "extra":
        built, made = take(2)
        new_out, new_ref = new_ref, made

    def load(which):
        if kind == "raw":
            k_ref, v_ref, q_ref, _ = tokens
            sources = [k_ref.at[0, 0], v_ref.at[0, 0], q_ref.at[0, 0]]
        else:
            sources = [tokens[which].at[i] for i in range(3)]
        return [
            pltpu.make_async_copy(sources[i], tok.at[i], sems.at[i]) for i in range(3)
        ]

    def run():
        if n_tokens == 2:
            for which in range(2):
                @pl.when(flags_ref[1] == which)
                def _():
                    for copy in load(which):
                        copy.start()
        else:
            for copy in load(0):
                copy.start()
        if kind == "extra":
            def bring(group):
                rows = 0
                copies = []
                for n, piece in enumerate(group):
                    height = piece.shape[1]
                    part = built.at[:, pl.ds(rows, height)]
                    copies.append(pltpu.make_async_copy(piece, part, sems.at[5 + n]))
                    rows += height
                for copy in copies:
                    copy.start()
                for copy in copies:
                    copy.wait()

            if n_states:
                @pl.when(flags_ref[2] != 0)
                def _():
                    bring(pieces)

                @pl.when(flags_ref[2] == 0)
                def _():
                    bring(states)
            else:
                bring(pieces)
            old = built
        else:
            old = states[0]
        if len(old.shape) == 4:
            old = old.at[0]
        waits = load(0)
        waits[0].wait()
        waits[1].wait()
        if kind == "raw":
            tok[1] = scaled_values(tokens[3][0, 0:1, :], tok[1])
        compute(tok, old, new_ref, acc, ans, block, waits[2].wait)
        target = ans_out.at[0, 0] if kind == "raw" else ans_out
        out = pltpu.make_async_copy(ans, target, sems.at[3])
        out.start()
        if kind == "extra":
            keep = pltpu.make_async_copy(made, new_out, sems.at[4])
            keep.start()
            keep.wait()
        out.wait()

    if kind == "extra":
        @pl.when(flags_ref[0] != 0)
        def _():
            run()
    else:
        run()


def unit(kind, flags, tokens, states, pieces, carry, hid, block=512):
    span, width = tokens[0].shape[-2:]
    scratch = [
        pltpu.VMEM((3, span, width), bf16),
        pltpu.VMEM((span, width), f32),
        pltpu.VMEM((span, width), bf16),
        pltpu.SemaphoreType.DMA((5 + len(pieces),)),
    ]
    if kind == "extra":
        scratch += [pltpu.VMEM((3, hid, width), bf16)] * 2
    kept = HBM if kind == "extra" else VMEM
    token_specs = [HBM] * len(tokens)
    if kind == "raw":
        token_specs[3] = VMEM
    n_tokens = 1 if kind == "raw" else len(tokens)
    call = pl.pallas_call(
        functools.partial(
            unit_kernel, kind, n_tokens, len(states), len(pieces), len(carry), block
        ),
        in_specs=[SMEM]
        + token_specs
        + [kept] * len(states)
        + [HBM] * len(pieces)
        + [VMEM] * len(carry),
        out_specs=[kept, HBM] + [VMEM] * len(carry),
        out_shape=[
            jax.ShapeDtypeStruct((3, hid, width), bf16),
            jax.ShapeDtypeStruct(
                tokens[0].shape if kind == "raw" else (span, width), bf16
            ),
        ]
        + [jax.ShapeDtypeStruct(c.shape, c.dtype) for c in carry],
        input_output_aliases={
            1 + len(tokens) + len(states) + len(pieces) + n: 2 + n
            for n in range(len(carry))
        },
        scratch_shapes=scratch,
        compiler_params=pltpu.CompilerParams(vmem_limit_bytes=LIMIT),
    )
    if kind == "raw":
        tokens = in_hbm(*tokens[:3]) + tokens[3:]
    return call(flags, *tokens, *states, *pieces, *carry)


def tied(value, *deps):
    return lax.optimization_barrier((value,) + deps)[0]


def body(fast_state, initial_fast, queries, token_keys, token_values, step_sizes):
    count = lax.axis_size("seq")
    position = lax.axis_index("seq")
    hid = fast_state.shape[2]
    i32 = jnp.int32
    first = (position == 0).astype(i32)
    second = (position == 1).astype(i32)
    extra = first + second
    flags = jnp.stack([extra, second, second])

    def send(value, pairs):
        return lax.ppermute(value, "seq", pairs)

    down = lambda t: [(s, s - t) for s in range(t, count)]
    up = lambda t: [(s, s + t) for s in range(count - t)]

    args = (token_keys, token_values, queries, step_sizes)
    pack1, pack2, pack3 = [pack(t, *args) for t in (1, 2, 3)]
    tokens1 = send(pack1, down(1))
    tokens2 = send(pack2, down(2))
    cross2 = send(pack2, [(1, 0), (0, 1)])
    tokens3 = send(pack3, down(3))
    cross3 = send(pack3, [(2, 0), (0, 1)])

    held = tied(initial_fast, pack3)
    chips = count // 2
    levels = []
    while chips > 1:
        radix = 4 if chips % 4 == 0 else 2
        chips //= radix
        levels.append((2 * chips, radix))

    def gather_level(value, stride, radix):
        return [
            send(value, [(j * stride + i, i) for i in range(stride)])
            for j in range(1, radix)
        ]

    got = gather_level(held, *levels[0])
    state, out = unit("raw", flags, list(args), [fast_state], [], [], hid)
    for level in levels[1:]:
        got = list(tied(tuple(got), out))
        held = jnp.concatenate([held] + got, axis=1)
        got = gather_level(held, *level)

    s1, a1 = unit("next", flags, [tokens1], [state], [], [], hid)
    b1 = send(a1, up(1))
    got = list(tied(tuple(got), a1))
    mine = [held] + got
    pieces = mine + [send(piece, [(0, 1), (1, 0)]) for piece in mine]
    e1, x1, s1 = unit("extra", flags, [pack1, cross2], [], pieces, [s1], hid)
    s2, a2 = unit("next", flags, [tokens2], [s1], [], [], hid)
    b2 = send(a2, up(2))
    e2, x2, s2 = unit("extra", flags, [cross2, pack3], [], [e1], [s2], hid)
    c2 = send(jnp.where(first != 0, x2, x1), [(0, 1), (1, 0)])
    _, x3, s2 = unit("extra", flags, [cross3], [e2], pieces, [s2], hid)
    c3 = send(x3, [(0, 2), (1, 0)])
    _, a3 = unit("next", flags, [tokens3], [s2], [], [], hid)
    b3 = send(a3, up(3))

    r1 = jnp.where(first != 0, x1, b1)
    r2 = jnp.where(extra != 0, c2, b2)
    early3 = jnp.where(second != 0, x2, c3)
    r3 = jnp.where(position < 3, early3, b3)
    for t, r in ((1, r1), (2, r2), (3, r3)):
        out = lax.dynamic_update_slice(out, r[None, None], (0, t, 0, 0))
    return out


def solution(mesh):
    return jax.shard_map(
        body,
        mesh=mesh,
        in_specs=(
            P(("grp", "seq"), None, None, None),
            P(None, "seq", None),
            P(("grp", "seq"), None, None, None),
            P(("grp", "seq"), None, None, None),
            P(("grp", "seq"), None, None, None),
            P(("grp", "seq"), None, None),
        ),
        out_specs=P(("grp", "seq"), None, None, None),
        check_vma=False,
    )
```

```python
import functools
import jax
import jax.numpy as jnp
from jax import lax
from jax.experimental import pallas as pl
from jax.experimental.pallas import tpu as pltpu
from jax.sharding import PartitionSpec as P

epsilon = 1e-06
f32 = jnp.float32
bf16 = jnp.bfloat16
HBM = pl.BlockSpec(memory_space=pltpu.HBM)
VMEM = pl.BlockSpec(memory_space=pltpu.VMEM)
SMEM = pl.BlockSpec(memory_space=pltpu.SMEM)
LIMIT = 28 << 20


def in_hbm(*arrays):
    return [pltpu.with_memory_space_constraint(a, pltpu.HBM) for a in arrays]


def nt(a, b):
    return lax.dot_general(a, b, (((1,), (1,)), ((), ())), preferred_element_type=f32)


def nn(a, b):
    return lax.dot_general(a, b, (((1,), (0,)), ((), ())), preferred_element_type=f32)


def sigmoid(x):
    return 0.5 * jnp.tanh(0.5 * x) + 0.5


def scaled_values(steps_row, values):
    lanes = 128
    span, width = values.shape
    column = jnp.broadcast_to(steps_row.astype(f32), (lanes, span)).T
    return jnp.concatenate(
        [
            (column * values[:, i : i + lanes].astype(f32)).astype(bf16)
            for i in range(0, width, lanes)
        ],
        axis=1,
    )


def pack_kernel(tick, k_ref, v_ref, q_ref, r_ref, o_ref, tok, sems):
    sources = (k_ref, v_ref, q_ref)
    loads = [
        pltpu.make_async_copy(sources[i].at[0, tick], tok.at[i], sems.at[i])
        for i in range(3)
    ]
    stores = [pltpu.make_async_copy(tok.at[i], o_ref.at[i], sems.at[3 + i]) for i in range(3)]
    for i in (1, 0, 2):
        loads[i].start()
    loads[1].wait()
    tok[1] = scaled_values(r_ref[0, tick : tick + 1, :], tok[1])
    stores[1].start()
    for i in (0, 2):
        loads[i].wait()
        stores[i].start()
    for store in stores:
        store.wait()


def pack(tick, keys, values, queries, steps):
    _, _, span, width = keys.shape
    return pl.pallas_call(
        functools.partial(pack_kernel, tick),
        in_specs=[HBM, HBM, HBM, VMEM],
        out_specs=HBM,
        out_shape=jax.ShapeDtypeStruct((3, span, width), bf16),
        scratch_shapes=[pltpu.VMEM((3, span, width), bf16), pltpu.SemaphoreType.DMA((6,))],
        compiler_params=pltpu.CompilerParams(vmem_limit_bytes=LIMIT),
    )(*in_hbm(keys, values, queries), steps)


def join_kernel(*refs):
    out = refs[-1]
    rows = 0
    for ref in refs[:-1]:
        height = ref.shape[1]
        out[:, rows : rows + height] = ref[...]
        rows += height


def join(parts):
    planes, _, width = parts[0].shape
    rows = sum(part.shape[1] for part in parts)
    return pl.pallas_call(
        join_kernel,
        in_specs=[VMEM] * len(parts),
        out_specs=VMEM,
        out_shape=jax.ShapeDtypeStruct((planes, rows, width), bf16),
        compiler_params=pltpu.CompilerParams(vmem_limit_bytes=LIMIT),
        name="join",
    )(*parts)


def step_rows(old, delta):
    previous = old.astype(f32)
    updated = previous + delta
    old_norm = jnp.sqrt(jnp.sum(previous * previous, axis=-1, keepdims=True) + epsilon)
    new_norm = jnp.sqrt(jnp.sum(updated * updated, axis=-1, keepdims=True) + epsilon)
    return (updated * (old_norm / new_norm)).astype(bf16)


def advance_rows(keys, target, gate, up, down):
    gate_pre = nt(gate, keys)
    up_pre = nt(up, keys)
    back_grad = nt(down, target)
    sig = sigmoid(gate_pre)
    silu = gate_pre * sig
    hidden = (silu * up_pre).astype(bf16)
    grad_up = (back_grad * silu).astype(bf16)
    grad_gate = ((back_grad * up_pre) * (sig * (1.0 + (gate_pre - silu)))).astype(bf16)
    return (
        step_rows(gate, nn(grad_gate, keys)),
        step_rows(up, nn(grad_up, keys)),
        step_rows(down, nn(hidden, target)),
    )


def serve_rows(queries, gate, up, down):
    c = nt(queries, gate)
    e = nt(queries, up)
    return nn((c * sigmoid(c) * e).astype(bf16), down)


def unit_kernel(tick, n_pieces, block, flags_ref, *refs):
    refs = list(refs)
    take = lambda n: [refs.pop(0) for _ in range(n)]
    tokens = take(4 if tick == 0 else 1)
    pieces = take(n_pieces)
    state, new_ref, ans_out, tok, acc, ans, sems = refs
    if tick == 0:
        sources = [tokens[i].at[0, 0] for i in range(3)]
        state = state.at[0]
    else:
        sources = [tokens[0].at[i] for i in range(3)]
        state = new_ref
    loads = [pltpu.make_async_copy(sources[i], tok.at[i], sems.at[i]) for i in range(3)]
    for load in loads:
        load.start()
    if n_pieces:
        @pl.when(flags_ref[tick] != 0)
        def _():
            rows = 0
            copies = []
            for n, piece in enumerate(pieces):
                height = piece.shape[1]
                part = new_ref.at[:, pl.ds(rows, height)]
                copies.append(pltpu.make_async_copy(piece, part, sems.at[4 + n]))
                rows += height
            for copy in copies:
                copy.start()
            for copy in copies:
                copy.wait()

    loads[0].wait()
    loads[1].wait()
    if tick == 0:
        tok[1] = scaled_values(tokens[3][0, 0:1, :], tok[1])
    count = new_ref.shape[1] // block
    for j in range(count):
        rows = pl.ds(j * block, block)
        new = advance_rows(tok[0], tok[1], state[0, rows], state[1, rows], state[2, rows])
        for i in range(3):
            new_ref[i, rows] = new[i]
        if j == 0:
            loads[2].wait()
        part = serve_rows(tok[2], new_ref[0, rows], new_ref[1, rows], new_ref[2, rows])
        total = part if j == 0 else acc[...] + part
        if j == count - 1:
            ans[...] = total.astype(bf16)
        else:
            acc[...] = total
    out = pltpu.make_async_copy(ans, ans_out.at[0, 0] if tick == 0 else ans_out, sems.at[3])
    out.start()
    out.wait()


def unit(tick, flags, tokens, state, pieces, block=512):
    span, width = tokens[0].shape[-2:]
    hid = state.shape[-2]
    token_specs = [HBM] * len(tokens)
    if tick == 0:
        token_specs[3] = VMEM
        tokens = in_hbm(*tokens[:3]) + tokens[3:]
    return pl.pallas_call(
        functools.partial(unit_kernel, tick, len(pieces), block),
        in_specs=[SMEM] + token_specs + [HBM] * len(pieces) + [VMEM],
        out_specs=[VMEM, HBM],
        out_shape=[
            jax.ShapeDtypeStruct((3, hid, width), bf16),
            jax.ShapeDtypeStruct(tokens[0].shape if tick == 0 else (span, width), bf16),
        ],
        input_output_aliases={} if tick == 0 else {1 + len(tokens) + len(pieces): 0},
        scratch_shapes=[
            pltpu.VMEM((3, span, width), bf16),
            pltpu.VMEM((span, width), f32),
            pltpu.VMEM((span, width), bf16),
            pltpu.SemaphoreType.DMA((4 + len(pieces),)),
        ],
        compiler_params=pltpu.CompilerParams(vmem_limit_bytes=LIMIT),
    )(flags, *tokens, *pieces, state)


def body(fast_state, initial_fast, queries, token_keys, token_values, step_sizes):
    count = lax.axis_size("seq")
    position = lax.axis_index("seq")
    ticks = token_keys.shape[1]
    flags = jnp.stack([(position + t == count).astype(jnp.int32) for t in range(ticks)])

    def send(value, pairs):
        return lax.ppermute(value, "seq", pairs)

    def shift(value, steps):
        return send(value, [(s, (s + steps) % count) for s in range(count)])

    args = [token_keys, token_values, queries, step_sizes]
    packs = [pack(t, *args) for t in range(1, ticks)]
    tokens = [shift(packs[t - 1], -t) for t in range(1, ticks)]

    last = 4
    width = count
    held = initial_fast
    while width > last:
        radix = 4 if width % (4 * last) == 0 else 2
        width //= radix
        base = count - width
        got = [
            send(held, [(base - j * width + i, base + i) for i in range(width)])
            for j in range(1, radix)
        ]
        held = join([held] + got)
    base = count - last
    swap = lambda value, bit: send(
        value, [(base + i, base + (i ^ bit)) for i in range(last)]
    )
    pieces = [held, swap(held, 2)]
    pieces += [swap(piece, 1) for piece in pieces]

    state, out = unit(0, flags, args, fast_state, [])
    answers = []
    for t in range(1, ticks):
        state, answer = unit(t, flags, [tokens[t - 1]], state, pieces)
        answers.append(shift(answer, t))
    for t in range(1, ticks):
        out = lax.dynamic_update_slice(out, answers[t - 1][None, None], (0, t, 0, 0))
    return out


def solution(mesh):
    return jax.shard_map(
        body,
        mesh=mesh,
        in_specs=(
            P(("grp", "seq"), None, None, None),
            P(None, "seq", None),
            P(("grp", "seq"), None, None, None),
            P(("grp", "seq"), None, None, None),
            P(("grp", "seq"), None, None, None),
            P(("grp", "seq"), None, None),
        ),
        out_specs=P(("grp", "seq"), None, None, None),
        check_vma=False,
    )
```

```python
import functools
import jax
import jax.numpy as jnp
from jax import lax
from jax.experimental import pallas as pl
from jax.experimental.pallas import tpu as pltpu
from jax.sharding import PartitionSpec as P

epsilon = 1e-06
f32 = jnp.float32
bf16 = jnp.bfloat16
HBM = pl.BlockSpec(memory_space=pltpu.HBM)
VMEM = pl.BlockSpec(memory_space=pltpu.VMEM)
SMEM = pl.BlockSpec(memory_space=pltpu.SMEM)
LIMIT = 28 << 20
EXTRA = -1


def in_hbm(*arrays):
    return [pltpu.with_memory_space_constraint(a, pltpu.HBM) for a in arrays]


def nt(a, b):
    return lax.dot_general(a, b, (((1,), (1,)), ((), ())), preferred_element_type=f32)


def nn(a, b):
    return lax.dot_general(a, b, (((1,), (0,)), ((), ())), preferred_element_type=f32)


def sigmoid(x):
    return 0.5 * jnp.tanh(0.5 * x) + 0.5


def scaled_values(steps_row, values):
    lanes = 128
    span, width = values.shape
    column = jnp.broadcast_to(steps_row.astype(f32), (lanes, span)).T
    return jnp.concatenate(
        [
            (column * values[:, i : i + lanes].astype(f32)).astype(bf16)
            for i in range(0, width, lanes)
        ],
        axis=1,
    )


def pack_kernel(tick, k_ref, v_ref, q_ref, r_ref, o_ref, tok, sems):
    sources = (k_ref, v_ref, q_ref)
    loads = [
        pltpu.make_async_copy(sources[i].at[0, tick], tok.at[i], sems.at[i])
        for i in range(3)
    ]
    stores = [pltpu.make_async_copy(tok.at[i], o_ref.at[i], sems.at[3 + i]) for i in range(3)]
    for i in (1, 0, 2):
        loads[i].start()
    loads[1].wait()
    tok[1] = scaled_values(r_ref[0, tick : tick + 1, :], tok[1])
    stores[1].start()
    for i in (0, 2):
        loads[i].wait()
        stores[i].start()
    for store in stores:
        store.wait()


def pack(tick, keys, values, queries, steps):
    _, _, span, width = keys.shape
    return pl.pallas_call(
        functools.partial(pack_kernel, tick),
        in_specs=[HBM, HBM, HBM, VMEM],
        out_specs=HBM,
        out_shape=jax.ShapeDtypeStruct((3, span, width), bf16),
        scratch_shapes=[pltpu.VMEM((3, span, width), bf16), pltpu.SemaphoreType.DMA((6,))],
        compiler_params=pltpu.CompilerParams(vmem_limit_bytes=LIMIT),
        cost_estimate=pl.CostEstimate(flops=0, bytes_accessed=0, transcendentals=0),
    )(*in_hbm(keys, values, queries), steps)


def join_kernel(*refs):
    out = refs[-1]
    rows = 0
    for ref in refs[:-1]:
        height = ref.shape[1]
        out[:, rows : rows + height] = ref[...]
        rows += height


def join(parts):
    planes, _, width = parts[0].shape
    rows = sum(part.shape[1] for part in parts)
    return pl.pallas_call(
        join_kernel,
        in_specs=[VMEM] * len(parts),
        out_specs=VMEM,
        out_shape=jax.ShapeDtypeStruct((planes, rows, width), bf16),
        compiler_params=pltpu.CompilerParams(vmem_limit_bytes=LIMIT),
        cost_estimate=pl.CostEstimate(flops=0, bytes_accessed=0, transcendentals=0),
        name="join",
    )(*parts)


def step_rows(old, delta):
    previous = old.astype(f32)
    updated = previous + delta
    old_norm = jnp.sqrt(jnp.sum(previous * previous, axis=-1, keepdims=True) + epsilon)
    new_norm = jnp.sqrt(jnp.sum(updated * updated, axis=-1, keepdims=True) + epsilon)
    return (updated * (old_norm / new_norm)).astype(bf16)


def advance_rows(keys, target, gate, up, down):
    gate_pre = nt(gate, keys)
    up_pre = nt(up, keys)
    back_grad = nt(down, target)
    sig = sigmoid(gate_pre)
    silu = gate_pre * sig
    hidden = (silu * up_pre).astype(bf16)
    grad_up = (back_grad * silu).astype(bf16)
    grad_gate = ((back_grad * up_pre) * (sig * (1.0 + (gate_pre - silu)))).astype(bf16)
    return (
        step_rows(gate, nn(grad_gate, keys)),
        step_rows(up, nn(grad_up, keys)),
        step_rows(down, nn(hidden, target)),
    )


def serve_rows(queries, gate, up, down):
    c = nt(queries, gate)
    e = nt(queries, up)
    return nn((c * sigmoid(c) * e).astype(bf16), down)


def unit_kernel(tick, n_pieces, block, flags_ref, *refs):
    refs = list(refs)
    take = lambda n: [refs.pop(0) for _ in range(n)]
    tokens = take(4 if tick == 0 else 1)
    pieces = take(n_pieces)
    if tick == EXTRA:
        ans_out, new_ref, tok, acc, ans, sems = refs

        @pl.when(flags_ref[0] != 0)
        def _():
            unit_steps(
                tick, block, flags_ref, tokens, pieces, new_ref, new_ref, ans_out, tok,
                acc, ans, sems,
            )
    else:
        unit_steps(tick, block, flags_ref, tokens, pieces, *refs)


def unit_steps(
    tick, block, flags_ref, tokens, pieces, state, new_ref, ans_out, tok, acc, ans, sems
):
    if tick == 0:
        sources = [tokens[i].at[0, 0] for i in range(3)]
        state = state.at[0]
    else:
        sources = [tokens[0].at[i] for i in range(3)]
        state = new_ref
    loads = [pltpu.make_async_copy(sources[i], tok.at[i], sems.at[i]) for i in range(3)]
    for load in loads:
        load.start()
    if pieces:
        @pl.when(flags_ref[max(tick, 0)] != 0)
        def _():
            rows = 0
            copies = []
            for n, piece in enumerate(pieces):
                height = piece.shape[1]
                part = new_ref.at[:, pl.ds(rows, height)]
                copies.append(pltpu.make_async_copy(piece, part, sems.at[4 + n]))
                rows += height
            for copy in copies:
                copy.start()
            for copy in copies:
                copy.wait()

    loads[0].wait()
    loads[1].wait()
    if tick == 0:
        tok[1] = scaled_values(tokens[3][0, 0:1, :], tok[1])
    count = new_ref.shape[1] // block

    def one(rows, first, last):
        new = advance_rows(tok[0], tok[1], state[0, rows], state[1, rows], state[2, rows])
        for i in range(3):
            new_ref[i, rows] = new[i]
        if first:
            loads[2].wait()
        part = serve_rows(tok[2], new_ref[0, rows], new_ref[1, rows], new_ref[2, rows])
        total = part if first else acc[...] + part
        if last:
            ans[...] = total.astype(bf16)
        else:
            acc[...] = total

    if tick == EXTRA:
        loads[2].wait()
        acc[...] = jnp.zeros_like(acc)

        @pl.loop(0, count)
        def _(j):
            one(pl.ds(pl.multiple_of(j * block, block), block), False, False)

        ans[...] = acc[...].astype(bf16)
    else:
        for j in range(count):
            one(pl.ds(j * block, block), j == 0, j == count - 1)
    out = pltpu.make_async_copy(ans, ans_out.at[0, 0] if tick == 0 else ans_out, sems.at[3])
    out.start()
    out.wait()


def unit(tick, flags, tokens, state, pieces, block=512):
    span, width = tokens[0].shape[-2:]
    if tick == EXTRA:
        hid = sum(piece.shape[1] for piece in pieces)
        states, state_shapes = [], []
        aliases = {}
    else:
        hid = state.shape[-2]
        states = [state]
        state_shapes = [jax.ShapeDtypeStruct((3, hid, width), bf16)]
        aliases = {} if tick == 0 else {1 + len(tokens) + len(pieces): 0}
    rows = [pltpu.VMEM((3, hid, width), bf16)] if tick == EXTRA else []
    token_specs = [HBM] * len(tokens)
    if tick == 0:
        token_specs[3] = VMEM
        tokens = in_hbm(*tokens[:3]) + tokens[3:]
    return pl.pallas_call(
        functools.partial(unit_kernel, tick, len(pieces), block),
        in_specs=[SMEM] + token_specs + [HBM] * len(pieces) + [VMEM] * len(states),
        out_specs=[VMEM] * len(states) + [HBM],
        out_shape=state_shapes
        + [jax.ShapeDtypeStruct(tokens[0].shape if tick == 0 else (span, width), bf16)],
        input_output_aliases=aliases,
        scratch_shapes=rows
        + [
            pltpu.VMEM((3, span, width), bf16),
            pltpu.VMEM((span, width), f32),
            pltpu.VMEM((span, width), bf16),
            pltpu.SemaphoreType.DMA((4 + len(pieces),)),
        ],
        compiler_params=pltpu.CompilerParams(vmem_limit_bytes=LIMIT),
        cost_estimate=pl.CostEstimate(flops=0, bytes_accessed=0, transcendentals=0),
    )(flags, *tokens, *pieces, *states)


def body(fast_state, initial_fast, queries, token_keys, token_values, step_sizes):
    count = lax.axis_size("seq")
    position = lax.axis_index("seq")
    ticks = token_keys.shape[1]
    flags = jnp.stack(
        [(position == count - 1).astype(jnp.int32)]
        + [
            ((position + t == count) & (t < ticks - 1)).astype(jnp.int32)
            for t in range(1, ticks)
        ]
    )

    def send(value, pairs):
        return lax.ppermute(value, "seq", pairs)

    def shift(value, steps):
        pairs = [(s, (s + steps) % count) for s in range(count)]
        if abs(steps) == ticks - 1:
            pairs = [p for p in pairs if set(p) != {0, count - steps if steps > 0 else count + steps}]
        return send(value, pairs)

    quads = count // 4
    cross = [(4 * q + c, 4 * q + c + 2) for q in range(quads) for c in (0, 1)]
    got = [send(initial_fast, cross)]
    held = initial_fast
    args = [token_keys, token_values, queries, step_sizes]
    packs = [pack(t, *args) for t in range(1, ticks)]
    tokens = [shift(packs[t - 1], -t) for t in range(1, ticks)]
    tokens_x = send(packs[-1], [(0, count - 1)])
    width = quads
    while width > 1:
        held = join([held] + got)
        radix = 4 if width % 4 == 0 else 2
        width //= radix
        base = quads - width
        got = [
            send(
                held,
                [
                    (4 * (base - j * width + i) + c, 4 * (base + i) + c)
                    for i in range(width)
                    for c in (2, 3)
                ],
            )
            for j in range(1, radix)
        ]
    held = join([held] + got)
    swapped = send(held, [(count - 2, count - 1), (count - 1, count - 2)])
    pieces = [held, swapped]

    state, out = unit(0, flags, args, fast_state, [])
    state, answer1 = unit(1, flags, tokens[:1], state, pieces)
    (answer_x,) = unit(EXTRA, flags, [tokens_x], None, pieces)
    back = [shift(answer1, 1)]
    for t in range(2, ticks):
        state, answer = unit(t, flags, tokens[t - 1 : t], state, pieces)
        back.append(shift(answer, t))
    back_x = send(answer_x, [(count - 1, 0)])
    back[-1] = jnp.where(position == 0, back_x, back[-1])
    for t in range(1, ticks):
        out = lax.dynamic_update_slice(out, back[t - 1][None, None], (0, t, 0, 0))
    return out


def solution(mesh):
    return jax.shard_map(
        body,
        mesh=mesh,
        in_specs=(
            P(("grp", "seq"), None, None, None),
            P(None, "seq", None),
            P(("grp", "seq"), None, None, None),
            P(("grp", "seq"), None, None, None),
            P(("grp", "seq"), None, None, None),
            P(("grp", "seq"), None, None),
        ),
        out_specs=P(("grp", "seq"), None, None, None),
        check_vma=False,
    )
```

```python
import functools
import jax
import jax.numpy as jnp
from jax import lax
from jax.experimental import pallas as pl
from jax.experimental.pallas import tpu as pltpu
from jax.sharding import PartitionSpec as P

epsilon = 1e-06
f32 = jnp.float32
bf16 = jnp.bfloat16
HBM = pl.BlockSpec(memory_space=pltpu.HBM)
VMEM = pl.BlockSpec(memory_space=pltpu.VMEM)
SMEM = pl.BlockSpec(memory_space=pltpu.SMEM)
LIMIT = 28 << 20
EXTRA = -1


def in_hbm(*arrays):
    return [pltpu.with_memory_space_constraint(a, pltpu.HBM) for a in arrays]


def nt(a, b):
    return lax.dot_general(a, b, (((1,), (1,)), ((), ())), preferred_element_type=f32)


def nn(a, b):
    return lax.dot_general(a, b, (((1,), (0,)), ((), ())), preferred_element_type=f32)


def sigmoid(x):
    return 0.5 * jnp.tanh(0.5 * x) + 0.5


def scaled_values(steps_row, values):
    lanes = 128
    span, width = values.shape
    column = jnp.broadcast_to(steps_row.astype(f32), (lanes, span)).T
    return jnp.concatenate(
        [
            (column * values[:, i : i + lanes].astype(f32)).astype(bf16)
            for i in range(0, width, lanes)
        ],
        axis=1,
    )


def pack_kernel(tick, k_ref, v_ref, q_ref, r_hbm, o_ref, tok, r_ref, sems):
    rates = pltpu.make_async_copy(r_hbm, r_ref, sems.at[6])
    rates.start()
    sources = (k_ref, v_ref, q_ref)
    loads = [
        pltpu.make_async_copy(sources[i].at[0, tick], tok.at[i], sems.at[i])
        for i in range(3)
    ]
    stores = [pltpu.make_async_copy(tok.at[i], o_ref.at[i], sems.at[3 + i]) for i in range(3)]
    for i in (1, 0, 2):
        loads[i].start()
    rates.wait()
    loads[1].wait()
    tok[1] = scaled_values(r_ref[0, tick : tick + 1, :], tok[1])
    stores[1].start()
    for i in (0, 2):
        loads[i].wait()
        stores[i].start()
    for store in stores:
        store.wait()


def pack(tick, keys, values, queries, steps):
    _, _, span, width = keys.shape
    return pl.pallas_call(
        functools.partial(pack_kernel, tick),
        in_specs=[HBM] * 4,
        out_specs=HBM,
        out_shape=jax.ShapeDtypeStruct((3, span, width), bf16),
        scratch_shapes=[
            pltpu.VMEM((3, span, width), bf16),
            pltpu.VMEM(steps.shape, bf16),
            pltpu.SemaphoreType.DMA((7,)),
        ],
        compiler_params=pltpu.CompilerParams(vmem_limit_bytes=LIMIT),
        cost_estimate=pl.CostEstimate(flops=0, bytes_accessed=0, transcendentals=0),
    )(*in_hbm(keys, values, queries, steps))


def join_kernel(*refs):
    out = refs[-1]
    rows = 0
    for ref in refs[:-1]:
        height = ref.shape[1]
        out[:, rows : rows + height] = ref[...]
        rows += height


def join(parts):
    planes, _, width = parts[0].shape
    rows = sum(part.shape[1] for part in parts)
    return pl.pallas_call(
        join_kernel,
        in_specs=[VMEM] * len(parts),
        out_specs=VMEM,
        out_shape=jax.ShapeDtypeStruct((planes, rows, width), bf16),
        compiler_params=pltpu.CompilerParams(vmem_limit_bytes=LIMIT),
        cost_estimate=pl.CostEstimate(flops=0, bytes_accessed=0, transcendentals=0),
        name="join",
    )(*parts)


def step_rows(old, delta):
    previous = old.astype(f32)
    updated = previous + delta
    old_norm = jnp.sqrt(jnp.sum(previous * previous, axis=-1, keepdims=True) + epsilon)
    new_norm = jnp.sqrt(jnp.sum(updated * updated, axis=-1, keepdims=True) + epsilon)
    return (updated * (old_norm / new_norm)).astype(bf16)


def advance_rows(keys, target, gate, up, down):
    gate_pre = nt(gate, keys)
    up_pre = nt(up, keys)
    back_grad = nt(down, target)
    sig = sigmoid(gate_pre)
    silu = gate_pre * sig
    hidden = (silu * up_pre).astype(bf16)
    grad_up = (back_grad * silu).astype(bf16)
    grad_gate = ((back_grad * up_pre) * (sig * (1.0 + (gate_pre - silu)))).astype(bf16)
    return (
        step_rows(gate, nn(grad_gate, keys)),
        step_rows(up, nn(grad_up, keys)),
        step_rows(down, nn(hidden, target)),
    )


def serve_rows(queries, gate, up, down):
    c = nt(queries, gate)
    e = nt(queries, up)
    return nn((c * sigmoid(c) * e).astype(bf16), down)


def unit_kernel(tick, n_pieces, block, flags_ref, *refs):
    refs = list(refs)
    take = lambda n: [refs.pop(0) for _ in range(n)]
    tokens = take(4 if tick == 0 else 1)
    pieces = take(n_pieces)
    if tick == EXTRA:
        ans_out, new_ref, tok, acc, ans, sems = refs

        @pl.when(flags_ref[0] != 0)
        def _():
            unit_steps(
                tick, block, flags_ref, tokens, pieces, new_ref, new_ref, ans_out, tok,
                acc, ans, sems,
            )
    else:
        unit_steps(tick, block, flags_ref, tokens, pieces, *refs)


def unit_steps(
    tick, block, flags_ref, tokens, pieces, state, new_ref, ans_out, tok, acc, ans, sems
):
    if tick == 0:
        sources = [tokens[i].at[0, 0] for i in range(3)]
        state = state.at[0]
    else:
        sources = [tokens[0].at[i] for i in range(3)]
        state = new_ref
    loads = [pltpu.make_async_copy(sources[i], tok.at[i], sems.at[i]) for i in range(3)]
    for load in loads:
        load.start()
    if pieces:
        @pl.when(flags_ref[max(tick, 0)] != 0)
        def _():
            rows = 0
            copies = []
            for n, piece in enumerate(pieces):
                height = piece.shape[1]
                part = new_ref.at[:, pl.ds(rows, height)]
                copies.append(pltpu.make_async_copy(piece, part, sems.at[4 + n]))
                rows += height
            for copy in copies:
                copy.start()
            for copy in copies:
                copy.wait()

    loads[0].wait()
    loads[1].wait()
    if tick == 0:
        tok[1] = scaled_values(tokens[3][0, 0:1, :], tok[1])
    count = new_ref.shape[1] // block

    def one(rows, first, last):
        new = advance_rows(tok[0], tok[1], state[0, rows], state[1, rows], state[2, rows])
        for i in range(3):
            new_ref[i, rows] = new[i]
        if first:
            loads[2].wait()
        part = serve_rows(tok[2], new_ref[0, rows], new_ref[1, rows], new_ref[2, rows])
        total = part if first else acc[...] + part
        if last:
            ans[...] = total.astype(bf16)
        else:
            acc[...] = total

    if tick == EXTRA:
        loads[2].wait()
        acc[...] = jnp.zeros_like(acc)

        @pl.loop(0, count)
        def _(j):
            one(pl.ds(pl.multiple_of(j * block, block), block), False, False)

        ans[...] = acc[...].astype(bf16)
    else:
        for j in range(count):
            one(pl.ds(j * block, block), j == 0, j == count - 1)
    out = pltpu.make_async_copy(ans, ans_out.at[0, 0] if tick == 0 else ans_out, sems.at[3])
    out.start()
    out.wait()


def unit(tick, flags, tokens, state, pieces, block=512):
    span, width = tokens[0].shape[-2:]
    if tick == EXTRA:
        hid = sum(piece.shape[1] for piece in pieces)
        states, state_shapes = [], []
        aliases = {}
    else:
        hid = state.shape[-2]
        states = [state]
        state_shapes = [jax.ShapeDtypeStruct((3, hid, width), bf16)]
        aliases = {} if tick == 0 else {1 + len(tokens) + len(pieces): 0}
    rows = [pltpu.VMEM((3, hid, width), bf16)] if tick == EXTRA else []
    token_specs = [HBM] * len(tokens)
    if tick == 0:
        token_specs[3] = VMEM
        tokens = in_hbm(*tokens[:3]) + tokens[3:]
    return pl.pallas_call(
        functools.partial(unit_kernel, tick, len(pieces), block),
        in_specs=[SMEM] + token_specs + [HBM] * len(pieces) + [VMEM] * len(states),
        out_specs=[VMEM] * len(states) + [HBM],
        out_shape=state_shapes
        + [jax.ShapeDtypeStruct(tokens[0].shape if tick == 0 else (span, width), bf16)],
        input_output_aliases=aliases,
        scratch_shapes=rows
        + [
            pltpu.VMEM((3, span, width), bf16),
            pltpu.VMEM((span, width), f32),
            pltpu.VMEM((span, width), bf16),
            pltpu.SemaphoreType.DMA((4 + len(pieces),)),
        ],
        compiler_params=pltpu.CompilerParams(vmem_limit_bytes=LIMIT),
        cost_estimate=pl.CostEstimate(flops=0, bytes_accessed=0, transcendentals=0),
    )(flags, *tokens, *pieces, *states)


def body(fast_state, initial_fast, queries, token_keys, token_values, step_sizes):
    count = lax.axis_size("seq")
    position = lax.axis_index("seq")
    ticks = token_keys.shape[1]
    flags = jnp.stack(
        [(position == count - 1).astype(jnp.int32)]
        + [
            ((position + t == count) & (t < ticks - 1)).astype(jnp.int32)
            for t in range(1, ticks)
        ]
    )

    def send(value, pairs):
        return lax.ppermute(value, "seq", pairs)

    def shift(value, steps):
        pairs = [(s, (s + steps) % count) for s in range(count)]
        if abs(steps) == ticks - 1:
            pairs = [p for p in pairs if set(p) != {0, count - steps if steps > 0 else count + steps}]
        return send(value, pairs)

    quads = count // 4
    cross = [(4 * q + c, 4 * q + c + 2) for q in range(quads) for c in (0, 1)]
    got = [send(initial_fast, cross)]
    held = initial_fast
    args = [token_keys, token_values, queries, step_sizes]
    packs = [pack(t, *args) for t in range(1, ticks)]
    tokens = [shift(packs[t - 1], -t) for t in range(1, ticks)]
    tokens_x = send(packs[-1], [(0, count - 1)])
    width = quads
    while width > 1:
        held = join([held] + got)
        radix = 4 if width % 4 == 0 else 2
        width //= radix
        base = quads - width
        got = [
            send(
                held,
                [
                    (4 * (base - j * width + i) + c, 4 * (base + i) + c)
                    for i in range(width)
                    for c in (2, 3)
                ],
            )
            for j in range(1, radix)
        ]
    held = join([held] + got)
    swapped = send(held, [(count - 2, count - 1), (count - 1, count - 2)])
    pieces = [held, swapped]

    state, out = unit(0, flags, args, fast_state, [])
    state, answer1 = unit(1, flags, tokens[:1], state, pieces)
    (answer_x,) = unit(EXTRA, flags, [tokens_x], None, in_hbm(*pieces))
    back = [shift(answer1, 1)]
    for t in range(2, ticks):
        restart = pieces if t < ticks - 1 else []
        state, answer = unit(t, flags, tokens[t - 1 : t], state, restart)
        if t == ticks - 2:
            state = keep(state)
        back.append(shift(answer, t))
    back_x = send(answer_x, [(count - 1, 0)])
    back[-1] = jnp.where(position == 0, back_x, back[-1])
    for t in range(1, ticks):
        out = lax.dynamic_update_slice(out, back[t - 1][None, None], (0, t, 0, 0))
    return out


def keep_kernel(state_ref, kept_ref):
    del state_ref, kept_ref


def keep(state):
    return pl.pallas_call(
        keep_kernel,
        in_specs=[VMEM],
        out_specs=VMEM,
        out_shape=jax.ShapeDtypeStruct(state.shape, state.dtype),
        input_output_aliases={0: 0},
        cost_estimate=pl.CostEstimate(flops=0, bytes_accessed=0, transcendentals=0),
        compiler_params=pltpu.CompilerParams(vmem_limit_bytes=1 << 20),
        name="keep",
    )(state)


def solution(mesh):
    return jax.shard_map(
        body,
        mesh=mesh,
        in_specs=(
            P(("grp", "seq"), None, None, None),
            P(None, "seq", None),
            P(("grp", "seq"), None, None, None),
            P(("grp", "seq"), None, None, None),
            P(("grp", "seq"), None, None, None),
            P(("grp", "seq"), None, None),
        ),
        out_specs=P(("grp", "seq"), None, None, None),
        check_vma=False,
    )
```

```python
import functools
import jax
import jax.numpy as jnp
from jax import lax
from jax.experimental import pallas as pl
from jax.experimental.pallas import tpu as pltpu
from jax.sharding import PartitionSpec as P

epsilon = 1e-06
f32 = jnp.float32
bf16 = jnp.bfloat16
HBM = pl.BlockSpec(memory_space=pltpu.HBM)
VMEM = pl.BlockSpec(memory_space=pltpu.VMEM)
SMEM = pl.BlockSpec(memory_space=pltpu.SMEM)
LIMIT = 28 << 20
EXTRA = -1


def in_hbm(*arrays):
    return [pltpu.with_memory_space_constraint(a, pltpu.HBM) for a in arrays]


def nt(a, b):
    return lax.dot_general(a, b, (((1,), (1,)), ((), ())), preferred_element_type=f32)


def nn(a, b):
    return lax.dot_general(a, b, (((1,), (0,)), ((), ())), preferred_element_type=f32)


def sigmoid(x):
    return 0.5 * jnp.tanh(0.5 * x) + 0.5


def scaled_values(steps_row, values):
    lanes = 128
    span, width = values.shape
    column = jnp.broadcast_to(steps_row.astype(f32), (lanes, span)).T
    return jnp.concatenate(
        [
            (column * values[:, i : i + lanes].astype(f32)).astype(bf16)
            for i in range(0, width, lanes)
        ],
        axis=1,
    )


def pack_kernel(tick, k_ref, v_ref, q_ref, r_hbm, o_ref, tok, r_ref, sems):
    rates = pltpu.make_async_copy(r_hbm, r_ref, sems.at[6])
    rates.start()
    sources = (k_ref, v_ref, q_ref)
    loads = [
        pltpu.make_async_copy(sources[i].at[0, tick], tok.at[i], sems.at[i])
        for i in range(3)
    ]
    stores = [pltpu.make_async_copy(tok.at[i], o_ref.at[i], sems.at[3 + i]) for i in range(3)]
    for i in (1, 0, 2):
        loads[i].start()
    rates.wait()
    loads[1].wait()
    tok[1] = scaled_values(r_ref[0, tick : tick + 1, :], tok[1])
    stores[1].start()
    for i in (0, 2):
        loads[i].wait()
        stores[i].start()
    for store in stores:
        store.wait()


def pack(tick, keys, values, queries, steps):
    _, _, span, width = keys.shape
    return pl.pallas_call(
        functools.partial(pack_kernel, tick),
        in_specs=[HBM] * 4,
        out_specs=HBM,
        out_shape=jax.ShapeDtypeStruct((3, span, width), bf16),
        scratch_shapes=[
            pltpu.VMEM((3, span, width), bf16),
            pltpu.VMEM(steps.shape, bf16),
            pltpu.SemaphoreType.DMA((7,)),
        ],
        compiler_params=pltpu.CompilerParams(vmem_limit_bytes=LIMIT),
        cost_estimate=pl.CostEstimate(flops=0, bytes_accessed=0, transcendentals=0),
    )(*in_hbm(keys, values, queries, steps))


def join_kernel(*refs):
    out = refs[-1]
    rows = 0
    for ref in refs[:-1]:
        height = ref.shape[1]
        out[:, rows : rows + height] = ref[...]
        rows += height


def join(parts):
    planes, _, width = parts[0].shape
    rows = sum(part.shape[1] for part in parts)
    return pl.pallas_call(
        join_kernel,
        in_specs=[VMEM] * len(parts),
        out_specs=VMEM,
        out_shape=jax.ShapeDtypeStruct((planes, rows, width), bf16),
        compiler_params=pltpu.CompilerParams(vmem_limit_bytes=LIMIT),
        cost_estimate=pl.CostEstimate(flops=0, bytes_accessed=0, transcendentals=0),
        name="join",
    )(*parts)


def step_rows(old, delta):
    previous = old.astype(f32)
    updated = previous + delta
    old_norm = jnp.sqrt(jnp.sum(previous * previous, axis=-1, keepdims=True) + epsilon)
    new_norm = jnp.sqrt(jnp.sum(updated * updated, axis=-1, keepdims=True) + epsilon)
    return (updated * (old_norm / new_norm)).astype(bf16)


def advance_rows(keys, target, gate, up, down):
    gate_pre = nt(gate, keys)
    up_pre = nt(up, keys)
    back_grad = nt(down, target)
    sig = sigmoid(gate_pre)
    silu = gate_pre * sig
    hidden = (silu * up_pre).astype(bf16)
    grad_up = (back_grad * silu).astype(bf16)
    grad_gate = ((back_grad * up_pre) * (sig * (1.0 + (gate_pre - silu)))).astype(bf16)
    return (
        step_rows(gate, nn(grad_gate, keys)),
        step_rows(up, nn(grad_up, keys)),
        step_rows(down, nn(hidden, target)),
    )


def serve_rows(queries, gate, up, down):
    c = nt(queries, gate)
    e = nt(queries, up)
    return nn((c * sigmoid(c) * e).astype(bf16), down)


def unit_kernel(tick, n_pieces, block, direct, flags_ref, *refs):
    refs = list(refs)
    take = lambda n: [refs.pop(0) for _ in range(n)]
    tokens = take(4 if tick == 0 else 1)
    pieces = take(n_pieces)
    if tick == EXTRA:
        ans_out, new_ref, tok, acc, ans, sems = refs

        @pl.when(flags_ref[0] != 0)
        def _():
            unit_steps(
                tick, block, flags_ref, tokens, pieces, new_ref, new_ref, ans_out, tok,
                acc, ans, sems,
            )
    elif direct:
        state, new_ref, ans_out, tok, acc, sems = refs
        unit_steps(
            tick, block, flags_ref, tokens, pieces, state, new_ref, ans_out, tok, acc,
            ans_out, sems,
        )
    else:
        unit_steps(tick, block, flags_ref, tokens, pieces, *refs)


def unit_steps(
    tick, block, flags_ref, tokens, pieces, state, new_ref, ans_out, tok, acc, ans, sems
):
    if tick == 0:
        sources = [tokens[i].at[0, 0] for i in range(3)]
        state = state.at[0]
    else:
        sources = [tokens[0].at[i] for i in range(3)]
        state = new_ref
    loads = [pltpu.make_async_copy(sources[i], tok.at[i], sems.at[i]) for i in range(3)]
    for load in loads:
        load.start()
    if pieces:
        @pl.when(flags_ref[max(tick, 0)] != 0)
        def _():
            rows = 0
            copies = []
            for n, piece in enumerate(pieces):
                height = piece.shape[1]
                part = new_ref.at[:, pl.ds(rows, height)]
                copies.append(pltpu.make_async_copy(piece, part, sems.at[4 + n]))
                rows += height
            for copy in copies:
                copy.start()
            for copy in copies:
                copy.wait()

    loads[0].wait()
    loads[1].wait()
    if tick == 0:
        tok[1] = scaled_values(tokens[3][0, 0:1, :], tok[1])
    count = new_ref.shape[1] // block

    def one(rows, first, last):
        new = advance_rows(tok[0], tok[1], state[0, rows], state[1, rows], state[2, rows])
        for i in range(3):
            new_ref[i, rows] = new[i]
        if first:
            loads[2].wait()
        part = serve_rows(tok[2], new_ref[0, rows], new_ref[1, rows], new_ref[2, rows])
        total = part if first else acc[...] + part
        if last:
            ans[...] = total.astype(bf16)
        else:
            acc[...] = total

    if tick == EXTRA:
        loads[2].wait()
        acc[...] = jnp.zeros_like(acc)

        @pl.loop(0, count)
        def _(j):
            one(pl.ds(pl.multiple_of(j * block, block), block), False, False)

        ans[...] = acc[...].astype(bf16)
    else:
        for j in range(count):
            one(pl.ds(j * block, block), j == 0, j == count - 1)
    if ans is not ans_out:
        target = ans_out.at[0, 0] if tick == 0 else ans_out
        out = pltpu.make_async_copy(ans, target, sems.at[3])
        out.start()
        out.wait()


def unit(tick, flags, tokens, state, pieces, block=512, direct=False):
    span, width = tokens[0].shape[-2:]
    if tick == EXTRA:
        hid = sum(piece.shape[1] for piece in pieces)
        states, state_shapes = [], []
        aliases = {}
    else:
        hid = state.shape[-2]
        states = [state]
        state_shapes = [jax.ShapeDtypeStruct((3, hid, width), bf16)]
        aliases = {} if tick == 0 else {1 + len(tokens) + len(pieces): 0}
    rows = [pltpu.VMEM((3, hid, width), bf16)] if tick == EXTRA else []
    token_specs = [HBM] * len(tokens)
    if tick == 0:
        token_specs[3] = VMEM
        tokens = in_hbm(*tokens[:3]) + tokens[3:]
    return pl.pallas_call(
        functools.partial(unit_kernel, tick, len(pieces), block, direct),
        in_specs=[SMEM] + token_specs + [HBM] * len(pieces) + [VMEM] * len(states),
        out_specs=[VMEM] * len(states) + [VMEM if direct else HBM],
        out_shape=state_shapes
        + [jax.ShapeDtypeStruct(tokens[0].shape if tick == 0 else (span, width), bf16)],
        input_output_aliases=aliases,
        scratch_shapes=rows
        + [
            pltpu.VMEM((3, span, width), bf16),
            pltpu.VMEM((span, width), f32),
        ]
        + ([] if direct else [pltpu.VMEM((span, width), bf16)])
        + [
            pltpu.SemaphoreType.DMA((4 + len(pieces),)),
        ],
        compiler_params=pltpu.CompilerParams(vmem_limit_bytes=LIMIT),
        cost_estimate=pl.CostEstimate(flops=0, bytes_accessed=0, transcendentals=0),
    )(flags, *tokens, *pieces, *states)


def body(fast_state, initial_fast, queries, token_keys, token_values, step_sizes):
    count = lax.axis_size("seq")
    position = lax.axis_index("seq")
    ticks = token_keys.shape[1]
    flags = jnp.stack(
        [(position == count - 1).astype(jnp.int32)]
        + [
            ((position + t == count) & (t < ticks - 1)).astype(jnp.int32)
            for t in range(1, ticks)
        ]
    )

    def send(value, pairs):
        return lax.ppermute(value, "seq", pairs)

    def shift(value, steps):
        pairs = [(s, (s + steps) % count) for s in range(count)]
        if abs(steps) == ticks - 1:
            pairs = [p for p in pairs if set(p) != {0, count - steps if steps > 0 else count + steps}]
        return send(value, pairs)

    quads = count // 4
    cross = [(4 * q + c, 4 * q + c + 2) for q in range(quads) for c in (0, 1)]
    got = [send(initial_fast, cross)]
    held = initial_fast
    args = [token_keys, token_values, queries, step_sizes]
    packs = [pack(t, *args) for t in range(1, ticks)]
    tokens = [shift(packs[t - 1], -t) for t in range(1, ticks)]
    tokens_x = send(packs[-1], [(0, count - 1)])
    width = quads
    while width > 1:
        held = join([held] + got)
        radix = 4 if width % 4 == 0 else 2
        width //= radix
        base = quads - width
        got = [
            send(
                held,
                [
                    (4 * (base - j * width + i) + c, 4 * (base + i) + c)
                    for i in range(width)
                    for c in (2, 3)
                ],
            )
            for j in range(1, radix)
        ]
    held = join([held] + got)
    swapped = send(held, [(count - 2, count - 1), (count - 1, count - 2)])
    pieces = [held, swapped]

    state, out = unit(0, flags, args, fast_state, [])
    state, answer1 = unit(1, flags, tokens[:1], state, pieces)
    (answer_x,) = unit(EXTRA, flags, [tokens_x], None, in_hbm(*pieces))
    back = [shift(answer1, 1)]
    for t in range(2, ticks):
        restart = pieces if t < ticks - 1 else []
        state, answer = unit(
            t, flags, tokens[t - 1 : t], state, restart, direct=t == ticks - 1
        )
        if t == ticks - 2:
            state = keep(state)
        back.append(shift(answer, t))
    back_x = send(answer_x, [(count - 1, 0)])
    back[-1] = jnp.where(position == 0, back_x, back[-1])
    for t in range(1, ticks):
        out = lax.dynamic_update_slice(out, back[t - 1][None, None], (0, t, 0, 0))
    return out


def keep_kernel(state_ref, kept_ref):
    del state_ref, kept_ref


def keep(state):
    return pl.pallas_call(
        keep_kernel,
        in_specs=[VMEM],
        out_specs=VMEM,
        out_shape=jax.ShapeDtypeStruct(state.shape, state.dtype),
        input_output_aliases={0: 0},
        cost_estimate=pl.CostEstimate(flops=0, bytes_accessed=0, transcendentals=0),
        compiler_params=pltpu.CompilerParams(vmem_limit_bytes=1 << 20),
        name="keep",
    )(state)


def solution(mesh):
    return jax.shard_map(
        body,
        mesh=mesh,
        in_specs=(
            P(("grp", "seq"), None, None, None),
            P(None, "seq", None),
            P(("grp", "seq"), None, None, None),
            P(("grp", "seq"), None, None, None),
            P(("grp", "seq"), None, None, None),
            P(("grp", "seq"), None, None),
        ),
        out_specs=P(("grp", "seq"), None, None, None),
        check_vma=False,
    )
```

```python
import functools
import jax
import jax.numpy as jnp
from jax import lax
from jax.experimental import pallas as pl
from jax.experimental.pallas import tpu as pltpu
from jax.sharding import PartitionSpec as P

epsilon = 1e-06
f32 = jnp.float32
bf16 = jnp.bfloat16
HBM = pl.BlockSpec(memory_space=pltpu.HBM)
VMEM = pl.BlockSpec(memory_space=pltpu.VMEM)
SMEM = pl.BlockSpec(memory_space=pltpu.SMEM)
LIMIT = 28 << 20
EXTRA = -1


def in_hbm(*arrays):
    return [pltpu.with_memory_space_constraint(a, pltpu.HBM) for a in arrays]


def nt(a, b):
    return lax.dot_general(a, b, (((1,), (1,)), ((), ())), preferred_element_type=f32)


def nn(a, b):
    return lax.dot_general(a, b, (((1,), (0,)), ((), ())), preferred_element_type=f32)


def sigmoid(x):
    return 0.5 * jnp.tanh(0.5 * x) + 0.5


def scaled_values(steps_row, values):
    lanes = 128
    span, width = values.shape
    column = jnp.broadcast_to(steps_row.astype(f32), (lanes, span)).T
    return jnp.concatenate(
        [
            (column * values[:, i : i + lanes].astype(f32)).astype(bf16)
            for i in range(0, width, lanes)
        ],
        axis=1,
    )


def pack_kernel(tick, split, k_ref, v_ref, q_ref, r_hbm, *refs):
    o_ref = refs[0]
    tok, r_ref, sems = refs[-3:]
    rates = pltpu.make_async_copy(r_hbm, r_ref, sems.at[6])
    rates.start()
    sources = (k_ref, v_ref, q_ref)
    loads = [
        pltpu.make_async_copy(sources[i].at[0, tick], tok.at[i], sems.at[i])
        for i in range(3)
    ]
    stores = [
        [pltpu.make_async_copy(tok.at[i], o_ref.at[i], sems.at[3 + i])] for i in range(3)
    ]
    if split:
        parts = (refs[1].at[0], refs[1].at[1], refs[2])
        for i in range(3):
            stores[i].append(pltpu.make_async_copy(tok.at[i], parts[i], sems.at[7 + i]))
    for i in (1, 0, 2):
        loads[i].start()
    rates.wait()
    loads[1].wait()
    tok[1] = scaled_values(r_ref[0, tick : tick + 1, :], tok[1])
    for i in (1, 0, 2):
        if i != 1:
            loads[i].wait()
        for store in reversed(stores[i]):
            store.start()
    for group in stores:
        for store in group:
            store.wait()


def pack(tick, keys, values, queries, steps):
    _, ticks, span, width = keys.shape
    split = tick == ticks - 1
    shapes = [(3, span, width)]
    if split:
        shapes += [(2, span, width), (span, width)]
    return pl.pallas_call(
        functools.partial(pack_kernel, tick, split),
        in_specs=[HBM] * 4,
        out_specs=[HBM] * len(shapes),
        out_shape=[jax.ShapeDtypeStruct(shape, bf16) for shape in shapes],
        scratch_shapes=[
            pltpu.VMEM((3, span, width), bf16),
            pltpu.VMEM(steps.shape, bf16),
            pltpu.SemaphoreType.DMA((10,)),
        ],
        compiler_params=pltpu.CompilerParams(vmem_limit_bytes=LIMIT),
        cost_estimate=pl.CostEstimate(flops=0, bytes_accessed=0, transcendentals=0),
    )(*in_hbm(keys, values, queries, steps))


def join_kernel(*refs):
    out = refs[-1]
    rows = 0
    for ref in refs[:-1]:
        height = ref.shape[1]
        out[:, rows : rows + height] = ref[...]
        rows += height


def join(parts):
    planes, _, width = parts[0].shape
    rows = sum(part.shape[1] for part in parts)
    return pl.pallas_call(
        join_kernel,
        in_specs=[VMEM] * len(parts),
        out_specs=VMEM,
        out_shape=jax.ShapeDtypeStruct((planes, rows, width), bf16),
        compiler_params=pltpu.CompilerParams(vmem_limit_bytes=LIMIT),
        cost_estimate=pl.CostEstimate(flops=0, bytes_accessed=0, transcendentals=0),
        name="join",
    )(*parts)


def step_rows(old, delta):
    previous = old.astype(f32)
    updated = previous + delta
    old_norm = jnp.sqrt(jnp.sum(previous * previous, axis=-1, keepdims=True) + epsilon)
    new_norm = jnp.sqrt(jnp.sum(updated * updated, axis=-1, keepdims=True) + epsilon)
    return (updated * (old_norm / new_norm)).astype(bf16)


def advance_rows(keys, target, gate, up, down):
    gate_pre = nt(gate, keys)
    up_pre = nt(up, keys)
    back_grad = nt(down, target)
    sig = sigmoid(gate_pre)
    silu = gate_pre * sig
    hidden = (silu * up_pre).astype(bf16)
    grad_up = (back_grad * silu).astype(bf16)
    grad_gate = ((back_grad * up_pre) * (sig * (1.0 + (gate_pre - silu)))).astype(bf16)
    return (
        step_rows(gate, nn(grad_gate, keys)),
        step_rows(up, nn(grad_up, keys)),
        step_rows(down, nn(hidden, target)),
    )


def serve_rows(queries, gate, up, down):
    c = nt(queries, gate)
    e = nt(queries, up)
    return nn((c * sigmoid(c) * e).astype(bf16), down)


def unit_kernel(tick, n_pieces, block, flags_ref, *refs):
    refs = list(refs)
    take = lambda n: [refs.pop(0) for _ in range(n)]
    tokens = take(4 if tick == 0 else 1)
    pieces = take(n_pieces)
    if tick == EXTRA:
        ans_out, new_ref, tok, acc, ans, sems = refs

        @pl.when(flags_ref[0] != 0)
        def _():
            unit_steps(
                tick, block, flags_ref, tokens, pieces, new_ref, new_ref, ans_out, tok,
                acc, ans, sems,
            )
    else:
        unit_steps(tick, block, flags_ref, tokens, pieces, *refs)


def unit_steps(
    tick, block, flags_ref, tokens, pieces, state, new_ref, ans_out, tok, acc, ans, sems
):
    if tick == 0:
        sources = [tokens[i].at[0, 0] for i in range(3)]
        state = state.at[0]
    else:
        sources = [tokens[0].at[i] for i in range(3)]
        state = new_ref
    loads = [pltpu.make_async_copy(sources[i], tok.at[i], sems.at[i]) for i in range(3)]
    for load in loads:
        load.start()
    if pieces:
        @pl.when(flags_ref[max(tick, 0)] != 0)
        def _():
            rows = 0
            copies = []
            for n, piece in enumerate(pieces):
                height = piece.shape[1]
                part = new_ref.at[:, pl.ds(rows, height)]
                copies.append(pltpu.make_async_copy(piece, part, sems.at[4 + n]))
                rows += height
            for copy in copies:
                copy.start()
            for copy in copies:
                copy.wait()

    loads[0].wait()
    loads[1].wait()
    if tick == 0:
        tok[1] = scaled_values(tokens[3][0, 0:1, :], tok[1])
    count = new_ref.shape[1] // block

    def one(rows, first, last):
        new = advance_rows(tok[0], tok[1], state[0, rows], state[1, rows], state[2, rows])
        for i in range(3):
            new_ref[i, rows] = new[i]
        if first:
            loads[2].wait()
        part = serve_rows(tok[2], new_ref[0, rows], new_ref[1, rows], new_ref[2, rows])
        total = part if first else acc[...] + part
        if last:
            ans[...] = total.astype(bf16)
        else:
            acc[...] = total

    if tick == EXTRA:
        loads[2].wait()
        acc[...] = jnp.zeros_like(acc)

        @pl.loop(0, count)
        def _(j):
            one(pl.ds(pl.multiple_of(j * block, block), block), False, False)

        ans[...] = acc[...].astype(bf16)
    else:
        for j in range(count):
            one(pl.ds(j * block, block), j == 0, j == count - 1)
    out = pltpu.make_async_copy(ans, ans_out.at[0, 0] if tick == 0 else ans_out, sems.at[3])
    out.start()
    out.wait()


def unit(tick, flags, tokens, state, pieces, block=512):
    span, width = tokens[0].shape[-2:]
    if tick == EXTRA:
        hid = sum(piece.shape[1] for piece in pieces)
        states, state_shapes = [], []
        aliases = {}
    else:
        hid = state.shape[-2]
        states = [state]
        state_shapes = [jax.ShapeDtypeStruct((3, hid, width), bf16)]
        aliases = {} if tick == 0 else {1 + len(tokens) + len(pieces): 0}
    rows = [pltpu.VMEM((3, hid, width), bf16)] if tick == EXTRA else []
    token_specs = [HBM] * len(tokens)
    if tick == 0:
        token_specs[3] = VMEM
        tokens = in_hbm(*tokens[:3]) + tokens[3:]
    return pl.pallas_call(
        functools.partial(unit_kernel, tick, len(pieces), block),
        in_specs=[SMEM] + token_specs + [HBM] * len(pieces) + [VMEM] * len(states),
        out_specs=[VMEM] * len(states) + [HBM],
        out_shape=state_shapes
        + [jax.ShapeDtypeStruct(tokens[0].shape if tick == 0 else (span, width), bf16)],
        input_output_aliases=aliases,
        scratch_shapes=rows
        + [
            pltpu.VMEM((3, span, width), bf16),
            pltpu.VMEM((span, width), f32),
            pltpu.VMEM((span, width), bf16),
            pltpu.SemaphoreType.DMA((4 + len(pieces),)),
        ],
        compiler_params=pltpu.CompilerParams(vmem_limit_bytes=LIMIT),
        cost_estimate=pl.CostEstimate(flops=0, bytes_accessed=0, transcendentals=0),
    )(flags, *tokens, *pieces, *states)


def body(fast_state, initial_fast, queries, token_keys, token_values, step_sizes):
    count = lax.axis_size("seq")
    position = lax.axis_index("seq")
    ticks = token_keys.shape[1]
    flags = jnp.stack(
        [(position == count - 1).astype(jnp.int32)]
        + [
            ((position + t == count) & (t < ticks - 1)).astype(jnp.int32)
            for t in range(1, ticks)
        ]
    )

    def send(value, pairs):
        return lax.ppermute(value, "seq", pairs)

    def shift(value, steps):
        pairs = [(s, (s + steps) % count) for s in range(count)]
        if abs(steps) == ticks - 1:
            pairs = [p for p in pairs if set(p) != {0, count - steps if steps > 0 else count + steps}]
        return send(value, pairs)

    quads = count // 4
    cross = [(4 * q + c, 4 * q + c + 2) for q in range(quads) for c in (0, 1)]
    got = [send(initial_fast, cross)]
    held = initial_fast
    args = [token_keys, token_values, queries, step_sizes]
    packs = [pack(t, *args) for t in range(1, ticks)]
    tokens = [shift(packs[t - 1][0], -t) for t in range(1, ticks - 1)]
    whole_last, learn_last, ask_last = packs[-1]
    learn_last = shift(learn_last, 1 - ticks)
    ask_last = shift(ask_last, 1 - ticks)
    tokens_x = send(whole_last, [(0, count - 1)])
    width = quads
    while width > 1:
        held = join([held] + got)
        radix = 4 if width % 4 == 0 else 2
        width //= radix
        base = quads - width
        got = [
            send(
                held,
                [
                    (4 * (base - j * width + i) + c, 4 * (base + i) + c)
                    for i in range(width)
                    for c in (2, 3)
                ],
            )
            for j in range(1, radix)
        ]
    held = join([held] + got)
    swapped = send(held, [(count - 2, count - 1), (count - 1, count - 2)])
    pieces = [held, swapped]

    state, out = unit(0, flags, args, fast_state, [])
    state, answer1 = unit(1, flags, tokens[:1], state, pieces)
    (answer_x,) = unit(EXTRA, flags, [tokens_x], None, in_hbm(*pieces))
    back = [shift(answer1, 1)]
    for t in range(2, ticks - 1):
        state, answer = unit(t, flags, tokens[t - 1 : t], state, pieces)
        if t == ticks - 2:
            state = keep(state)
        back.append(shift(answer, t))
    state = advance_only(learn_last, state)
    back.append(shift(serve_only(ask_last, state), ticks - 1))
    back_x = send(answer_x, [(count - 1, 0)])
    back[-1] = jnp.where(position == 0, back_x, back[-1])
    for t in range(1, ticks):
        out = lax.dynamic_update_slice(out, back[t - 1][None, None], (0, t, 0, 0))
    return out


def advance_kernel(block, tokens_ref, state_ref, new_ref, tok, sems):
    del state_ref
    loads = [
        pltpu.make_async_copy(tokens_ref.at[i], tok.at[i], sems.at[i]) for i in range(2)
    ]
    for load in loads:
        load.start()
    for load in loads:
        load.wait()
    for j in range(new_ref.shape[1] // block):
        rows = pl.ds(j * block, block)
        new = advance_rows(
            tok[0], tok[1], new_ref[0, rows], new_ref[1, rows], new_ref[2, rows]
        )
        for i in range(3):
            new_ref[i, rows] = new[i]


def advance_only(tokens, state, block=512):
    return pl.pallas_call(
        functools.partial(advance_kernel, block),
        in_specs=[HBM, VMEM],
        out_specs=VMEM,
        out_shape=jax.ShapeDtypeStruct(state.shape, bf16),
        input_output_aliases={1: 0},
        scratch_shapes=[pltpu.VMEM(tokens.shape, bf16), pltpu.SemaphoreType.DMA((2,))],
        compiler_params=pltpu.CompilerParams(vmem_limit_bytes=LIMIT),
        cost_estimate=pl.CostEstimate(flops=0, bytes_accessed=0, transcendentals=0),
        name="advance",
    )(tokens, state)


def serve_kernel(block, queries_ref, state_ref, ans_ref, asked, acc, sem):
    load = pltpu.make_async_copy(queries_ref, asked, sem)
    load.start()
    load.wait()
    count = state_ref.shape[1] // block
    for j in range(count):
        rows = pl.ds(j * block, block)
        part = serve_rows(
            asked[...], state_ref[0, rows], state_ref[1, rows], state_ref[2, rows]
        )
        total = part if j == 0 else acc[...] + part
        if j == count - 1:
            ans_ref[...] = total.astype(bf16)
        else:
            acc[...] = total


def serve_only(queries, state, block=512):
    return pl.pallas_call(
        functools.partial(serve_kernel, block),
        in_specs=[HBM, VMEM],
        out_specs=VMEM,
        out_shape=jax.ShapeDtypeStruct(queries.shape, bf16),
        scratch_shapes=[
            pltpu.VMEM(queries.shape, bf16),
            pltpu.VMEM(queries.shape, f32),
            pltpu.SemaphoreType.DMA,
        ],
        compiler_params=pltpu.CompilerParams(vmem_limit_bytes=LIMIT),
        cost_estimate=pl.CostEstimate(flops=0, bytes_accessed=0, transcendentals=0),
        name="serve",
    )(queries, state)


def keep_kernel(state_ref, kept_ref):
    del state_ref, kept_ref


def keep(state):
    return pl.pallas_call(
        keep_kernel,
        in_specs=[VMEM],
        out_specs=VMEM,
        out_shape=jax.ShapeDtypeStruct(state.shape, state.dtype),
        input_output_aliases={0: 0},
        cost_estimate=pl.CostEstimate(flops=0, bytes_accessed=0, transcendentals=0),
        compiler_params=pltpu.CompilerParams(vmem_limit_bytes=1 << 20),
        name="keep",
    )(state)


def solution(mesh):
    return jax.shard_map(
        body,
        mesh=mesh,
        in_specs=(
            P(("grp", "seq"), None, None, None),
            P(None, "seq", None),
            P(("grp", "seq"), None, None, None),
            P(("grp", "seq"), None, None, None),
            P(("grp", "seq"), None, None, None),
            P(("grp", "seq"), None, None),
        ),
        out_specs=P(("grp", "seq"), None, None, None),
        check_vma=False,
    )
```

```python
import functools
import jax
import jax.numpy as jnp
from jax import lax
from jax.experimental import pallas as pl
from jax.experimental.pallas import tpu as pltpu
from jax.sharding import PartitionSpec as P

epsilon = 1e-06
f32 = jnp.float32
bf16 = jnp.bfloat16
HBM = pl.BlockSpec(memory_space=pltpu.HBM)
VMEM = pl.BlockSpec(memory_space=pltpu.VMEM)
SMEM = pl.BlockSpec(memory_space=pltpu.SMEM)
LIMIT = 28 << 20
EXTRA = -1


def in_hbm(*arrays):
    return [pltpu.with_memory_space_constraint(a, pltpu.HBM) for a in arrays]


def nt(a, b):
    return lax.dot_general(a, b, (((1,), (1,)), ((), ())), preferred_element_type=f32)


def nn(a, b):
    return lax.dot_general(a, b, (((1,), (0,)), ((), ())), preferred_element_type=f32)


def sigmoid(x):
    return 0.5 * jnp.tanh(0.5 * x) + 0.5


def scaled_values(steps_row, values):
    lanes = 128
    span, width = values.shape
    column = jnp.broadcast_to(steps_row.astype(f32), (lanes, span)).T
    return jnp.concatenate(
        [
            (column * values[:, i : i + lanes].astype(f32)).astype(bf16)
            for i in range(0, width, lanes)
        ],
        axis=1,
    )


def pack_kernel(tick, split, k_ref, v_ref, q_ref, r_hbm, *refs):
    o_ref = refs[0]
    tok, r_ref, sems = refs[-3:]
    rates = pltpu.make_async_copy(r_hbm, r_ref, sems.at[6])
    rates.start()
    sources = (k_ref, v_ref, q_ref)
    loads = [
        pltpu.make_async_copy(sources[i].at[0, tick], tok.at[i], sems.at[i])
        for i in range(3)
    ]
    stores = [
        [pltpu.make_async_copy(tok.at[i], o_ref.at[i], sems.at[3 + i])] for i in range(3)
    ]
    if split:
        parts = (refs[1].at[0], refs[1].at[1], refs[2])
        for i in range(3):
            stores[i].append(pltpu.make_async_copy(tok.at[i], parts[i], sems.at[7 + i]))
    for i in (1, 0, 2):
        loads[i].start()
    rates.wait()
    loads[1].wait()
    tok[1] = scaled_values(r_ref[0, tick : tick + 1, :], tok[1])
    for i in (1, 0, 2):
        if i != 1:
            loads[i].wait()
        for store in reversed(stores[i]):
            store.start()
    for group in stores:
        for store in group:
            store.wait()


def pack(tick, keys, values, queries, steps):
    _, ticks, span, width = keys.shape
    split = tick == ticks - 1
    shapes = [(3, span, width)]
    if split:
        shapes += [(2, span, width), (span, width)]
    return pl.pallas_call(
        functools.partial(pack_kernel, tick, split),
        in_specs=[HBM] * 4,
        out_specs=[HBM] * len(shapes),
        out_shape=[jax.ShapeDtypeStruct(shape, bf16) for shape in shapes],
        scratch_shapes=[
            pltpu.VMEM((3, span, width), bf16),
            pltpu.VMEM(steps.shape, bf16),
            pltpu.SemaphoreType.DMA((10,)),
        ],
        compiler_params=pltpu.CompilerParams(vmem_limit_bytes=LIMIT),
        cost_estimate=pl.CostEstimate(flops=0, bytes_accessed=0, transcendentals=0),
    )(*in_hbm(keys, values, queries, steps))


def join_kernel(*refs):
    out = refs[-1]
    rows = 0
    for ref in refs[:-1]:
        height = ref.shape[1]
        out[:, rows : rows + height] = ref[...]
        rows += height


def join(parts):
    planes, _, width = parts[0].shape
    rows = sum(part.shape[1] for part in parts)
    return pl.pallas_call(
        join_kernel,
        in_specs=[VMEM] * len(parts),
        out_specs=VMEM,
        out_shape=jax.ShapeDtypeStruct((planes, rows, width), bf16),
        compiler_params=pltpu.CompilerParams(vmem_limit_bytes=LIMIT),
        cost_estimate=pl.CostEstimate(flops=0, bytes_accessed=0, transcendentals=0),
        name="join",
    )(*parts)


def step_rows(old, delta):
    previous = old.astype(f32)
    updated = previous + delta
    old_norm = jnp.sqrt(jnp.sum(previous * previous, axis=-1, keepdims=True) + epsilon)
    new_norm = jnp.sqrt(jnp.sum(updated * updated, axis=-1, keepdims=True) + epsilon)
    return (updated * (old_norm / new_norm)).astype(bf16)


def advance_rows(keys, target, gate, up, down):
    gate_pre = nt(gate, keys)
    up_pre = nt(up, keys)
    back_grad = nt(down, target)
    sig = sigmoid(gate_pre)
    silu = gate_pre * sig
    hidden = (silu * up_pre).astype(bf16)
    grad_up = (back_grad * silu).astype(bf16)
    grad_gate = ((back_grad * up_pre) * (sig * (1.0 + (gate_pre - silu)))).astype(bf16)
    return (
        step_rows(gate, nn(grad_gate, keys)),
        step_rows(up, nn(grad_up, keys)),
        step_rows(down, nn(hidden, target)),
    )


def serve_rows(queries, gate, up, down):
    c = nt(queries, gate)
    e = nt(queries, up)
    return nn((c * sigmoid(c) * e).astype(bf16), down)


def unit_kernel(tick, n_pieces, block, flags_ref, *refs):
    refs = list(refs)
    take = lambda n: [refs.pop(0) for _ in range(n)]
    tokens = take(4 if tick == 0 else 1)
    pieces = take(n_pieces)
    if tick == EXTRA:
        ans_out, new_ref, tok, acc, ans, sems = refs

        @pl.when(flags_ref[0] != 0)
        def _():
            unit_steps(
                tick, block, flags_ref, tokens, pieces, new_ref, new_ref, ans_out, tok,
                acc, ans, sems,
            )
    else:
        unit_steps(tick, block, flags_ref, tokens, pieces, *refs)


def unit_steps(
    tick, block, flags_ref, tokens, pieces, state, new_ref, ans_out, tok, acc, ans, sems
):
    if tick == 0:
        sources = [tokens[i].at[0, 0] for i in range(3)]
        state = state.at[0]
    else:
        sources = [tokens[0].at[i] for i in range(3)]
        state = new_ref
    loads = [pltpu.make_async_copy(sources[i], tok.at[i], sems.at[i]) for i in range(3)]
    for load in loads:
        load.start()
    if pieces:
        @pl.when(flags_ref[max(tick, 0)] != 0)
        def _():
            rows = 0
            copies = []
            for n, piece in enumerate(pieces):
                height = piece.shape[1]
                part = new_ref.at[:, pl.ds(rows, height)]
                copies.append(pltpu.make_async_copy(piece, part, sems.at[4 + n]))
                rows += height
            for copy in copies:
                copy.start()
            for copy in copies:
                copy.wait()

    loads[0].wait()
    loads[1].wait()
    if tick == 0:
        tok[1] = scaled_values(tokens[3][0, 0:1, :], tok[1])
    count = new_ref.shape[1] // block

    def one(rows, first, last):
        new = advance_rows(tok[0], tok[1], state[0, rows], state[1, rows], state[2, rows])
        for i in range(3):
            new_ref[i, rows] = new[i]
        if first:
            loads[2].wait()
        part = serve_rows(tok[2], new_ref[0, rows], new_ref[1, rows], new_ref[2, rows])
        total = part if first else acc[...] + part
        if last:
            ans[...] = total.astype(bf16)
        else:
            acc[...] = total

    for j in range(count):
        one(pl.ds(j * block, block), j == 0, j == count - 1)
    out = pltpu.make_async_copy(ans, ans_out.at[0, 0] if tick == 0 else ans_out, sems.at[3])
    out.start()
    out.wait()


def unit(tick, flags, tokens, state, pieces, block=512):
    span, width = tokens[0].shape[-2:]
    if tick == EXTRA:
        hid = sum(piece.shape[1] for piece in pieces)
        states, state_shapes = [], []
        aliases = {}
    else:
        hid = state.shape[-2]
        states = [state]
        state_shapes = [jax.ShapeDtypeStruct((3, hid, width), bf16)]
        aliases = {} if tick == 0 else {1 + len(tokens) + len(pieces): 0}
    rows = [pltpu.VMEM((3, hid, width), bf16)] if tick == EXTRA else []
    token_specs = [HBM] * len(tokens)
    if tick == 0:
        token_specs[3] = VMEM
        tokens = in_hbm(*tokens[:3]) + tokens[3:]
    return pl.pallas_call(
        functools.partial(unit_kernel, tick, len(pieces), block),
        in_specs=[SMEM] + token_specs + [HBM] * len(pieces) + [VMEM] * len(states),
        out_specs=[VMEM] * len(states) + [HBM],
        out_shape=state_shapes
        + [jax.ShapeDtypeStruct(tokens[0].shape if tick == 0 else (span, width), bf16)],
        input_output_aliases=aliases,
        scratch_shapes=rows
        + [
            pltpu.VMEM((3, span, width), bf16),
            pltpu.VMEM((span, width), f32),
            pltpu.VMEM((span, width), bf16),
            pltpu.SemaphoreType.DMA((4 + len(pieces),)),
        ],
        compiler_params=pltpu.CompilerParams(vmem_limit_bytes=LIMIT),
        cost_estimate=pl.CostEstimate(flops=0, bytes_accessed=0, transcendentals=0),
    )(flags, *tokens, *pieces, *states)


def body(fast_state, initial_fast, queries, token_keys, token_values, step_sizes):
    count = lax.axis_size("seq")
    position = lax.axis_index("seq")
    ticks = token_keys.shape[1]
    flags = jnp.stack(
        [(position == count - 1).astype(jnp.int32)]
        + [
            ((position + t == count) & (t < ticks - 1)).astype(jnp.int32)
            for t in range(1, ticks)
        ]
    )

    def send(value, pairs):
        return lax.ppermute(value, "seq", pairs)

    def shift(value, steps):
        pairs = [(s, (s + steps) % count) for s in range(count)]
        if abs(steps) == ticks - 1:
            pairs = [p for p in pairs if set(p) != {0, count - steps if steps > 0 else count + steps}]
        return send(value, pairs)

    quads = count // 4
    cross = [(4 * q + c, 4 * q + c + 2) for q in range(quads) for c in (0, 1)]
    got = [send(initial_fast, cross)]
    held = initial_fast
    args = [token_keys, token_values, queries, step_sizes]
    packs = [pack(t, *args) for t in range(1, ticks)]
    tokens = [shift(packs[t - 1][0], -t) for t in range(1, ticks - 1)]
    whole_last, learn_last, ask_last = packs[-1]
    learn_last = shift(learn_last, 1 - ticks)
    ask_last = shift(ask_last, 1 - ticks)
    tokens_x = send(whole_last, [(0, count - 1)])
    width = quads
    while width > 1:
        held = join([held] + got)
        radix = 4 if width % 4 == 0 else 2
        width //= radix
        base = quads - width
        got = [
            send(
                held,
                [
                    (4 * (base - j * width + i) + c, 4 * (base + i) + c)
                    for i in range(width)
                    for c in (2, 3)
                ],
            )
            for j in range(1, radix)
        ]
    held = join([held] + got)
    swapped = send(held, [(count - 2, count - 1), (count - 1, count - 2)])
    pieces = [held, swapped]

    state, out = unit(0, flags, args, fast_state, [])
    state, answer1 = unit(1, flags, tokens[:1], state, pieces)
    (answer_x,) = unit(EXTRA, flags, [tokens_x], None, in_hbm(*pieces))
    back = [shift(answer1, 1)]
    for t in range(2, ticks - 1):
        state, answer = unit(t, flags, tokens[t - 1 : t], state, pieces)
        if t == ticks - 2:
            state = keep(state)
        back.append(shift(answer, t))
    state = advance_only(learn_last, state)
    back.append(shift(serve_only(ask_last, state), ticks - 1))
    back_x = send(answer_x, [(count - 1, 0)])
    back[-1] = jnp.where(position == 0, back_x, back[-1])
    for t in range(1, ticks):
        out = lax.dynamic_update_slice(out, back[t - 1][None, None], (0, t, 0, 0))
    return out


def advance_kernel(block, tokens_ref, state_ref, new_ref, tok, sems):
    del state_ref
    loads = [
        pltpu.make_async_copy(tokens_ref.at[i], tok.at[i], sems.at[i]) for i in range(2)
    ]
    for load in loads:
        load.start()
    for load in loads:
        load.wait()
    for j in range(new_ref.shape[1] // block):
        rows = pl.ds(j * block, block)
        new = advance_rows(
            tok[0], tok[1], new_ref[0, rows], new_ref[1, rows], new_ref[2, rows]
        )
        for i in range(3):
            new_ref[i, rows] = new[i]


def advance_only(tokens, state, block=512):
    return pl.pallas_call(
        functools.partial(advance_kernel, block),
        in_specs=[HBM, VMEM],
        out_specs=VMEM,
        out_shape=jax.ShapeDtypeStruct(state.shape, bf16),
        input_output_aliases={1: 0},
        scratch_shapes=[pltpu.VMEM(tokens.shape, bf16), pltpu.SemaphoreType.DMA((2,))],
        compiler_params=pltpu.CompilerParams(vmem_limit_bytes=LIMIT),
        cost_estimate=pl.CostEstimate(flops=0, bytes_accessed=0, transcendentals=0),
        name="advance",
    )(tokens, state)


def serve_kernel(block, queries_ref, state_ref, ans_ref, asked, acc, sem):
    load = pltpu.make_async_copy(queries_ref, asked, sem)
    load.start()
    load.wait()
    count = state_ref.shape[1] // block
    for j in range(count):
        rows = pl.ds(j * block, block)
        part = serve_rows(
            asked[...], state_ref[0, rows], state_ref[1, rows], state_ref[2, rows]
        )
        total = part if j == 0 else acc[...] + part
        if j == count - 1:
            ans_ref[...] = total.astype(bf16)
        else:
            acc[...] = total


def serve_only(queries, state, block=512):
    return pl.pallas_call(
        functools.partial(serve_kernel, block),
        in_specs=[HBM, VMEM],
        out_specs=VMEM,
        out_shape=jax.ShapeDtypeStruct(queries.shape, bf16),
        scratch_shapes=[
            pltpu.VMEM(queries.shape, bf16),
            pltpu.VMEM(queries.shape, f32),
            pltpu.SemaphoreType.DMA,
        ],
        compiler_params=pltpu.CompilerParams(vmem_limit_bytes=LIMIT),
        cost_estimate=pl.CostEstimate(flops=0, bytes_accessed=0, transcendentals=0),
        name="serve",
    )(queries, state)


def keep_kernel(state_ref, kept_ref):
    del state_ref, kept_ref


def keep(state):
    return pl.pallas_call(
        keep_kernel,
        in_specs=[VMEM],
        out_specs=VMEM,
        out_shape=jax.ShapeDtypeStruct(state.shape, state.dtype),
        input_output_aliases={0: 0},
        cost_estimate=pl.CostEstimate(flops=0, bytes_accessed=0, transcendentals=0),
        compiler_params=pltpu.CompilerParams(vmem_limit_bytes=1 << 20),
        name="keep",
    )(state)


def solution(mesh):
    return jax.shard_map(
        body,
        mesh=mesh,
        in_specs=(
            P(("grp", "seq"), None, None, None),
            P(None, "seq", None),
            P(("grp", "seq"), None, None, None),
            P(("grp", "seq"), None, None, None),
            P(("grp", "seq"), None, None, None),
            P(("grp", "seq"), None, None),
        ),
        out_specs=P(("grp", "seq"), None, None, None),
        check_vma=False,
    )
```

```python
import functools
import jax
import jax.numpy as jnp
from jax import lax
from jax.experimental import pallas as pl
from jax.experimental.pallas import tpu as pltpu
from jax.sharding import PartitionSpec as P

epsilon = 1e-06
f32 = jnp.float32
bf16 = jnp.bfloat16
HBM = pl.BlockSpec(memory_space=pltpu.HBM)
VMEM = pl.BlockSpec(memory_space=pltpu.VMEM)
SMEM = pl.BlockSpec(memory_space=pltpu.SMEM)
LIMIT = 28 << 20
EXTRA = -1


def in_hbm(*arrays):
    return [pltpu.with_memory_space_constraint(a, pltpu.HBM) for a in arrays]


def nt(a, b):
    return lax.dot_general(a, b, (((1,), (1,)), ((), ())), preferred_element_type=f32)


def nn(a, b):
    return lax.dot_general(a, b, (((1,), (0,)), ((), ())), preferred_element_type=f32)


def sigmoid(x):
    return 0.5 * jnp.tanh(0.5 * x) + 0.5


def scaled_values(steps_row, values):
    lanes = 128
    span, width = values.shape
    column = jnp.broadcast_to(steps_row.astype(f32), (lanes, span)).T
    return jnp.concatenate(
        [
            (column * values[:, i : i + lanes].astype(f32)).astype(bf16)
            for i in range(0, width, lanes)
        ],
        axis=1,
    )


def pack_kernel(tick, split, k_ref, v_ref, q_ref, r_hbm, *refs):
    o_ref = refs[0]
    tok, r_ref, sems = refs[-3:]
    rates = pltpu.make_async_copy(r_hbm, r_ref, sems.at[6])
    rates.start()
    sources = (k_ref, v_ref, q_ref)
    loads = [
        pltpu.make_async_copy(sources[i].at[0, tick], tok.at[i], sems.at[i])
        for i in range(3)
    ]
    stores = [
        [pltpu.make_async_copy(tok.at[i], o_ref.at[i], sems.at[3 + i])] for i in range(3)
    ]
    if split:
        parts = (refs[1].at[0], refs[1].at[1], refs[2])
        for i in range(3):
            stores[i].append(pltpu.make_async_copy(tok.at[i], parts[i], sems.at[7 + i]))
    for i in (1, 0, 2):
        loads[i].start()
    rates.wait()
    loads[1].wait()
    tok[1] = scaled_values(r_ref[0, tick : tick + 1, :], tok[1])
    for i in (1, 0, 2):
        if i != 1:
            loads[i].wait()
        for store in reversed(stores[i]):
            store.start()
    for group in stores:
        for store in group:
            store.wait()


def pack(tick, keys, values, queries, steps):
    _, ticks, span, width = keys.shape
    split = tick == ticks - 1
    shapes = [(3, span, width)]
    if split:
        shapes += [(2, span, width), (span, width)]
    return pl.pallas_call(
        functools.partial(pack_kernel, tick, split),
        in_specs=[HBM] * 4,
        out_specs=[HBM] * len(shapes),
        out_shape=[jax.ShapeDtypeStruct(shape, bf16) for shape in shapes],
        scratch_shapes=[
            pltpu.VMEM((3, span, width), bf16),
            pltpu.VMEM(steps.shape, bf16),
            pltpu.SemaphoreType.DMA((10,)),
        ],
        compiler_params=pltpu.CompilerParams(vmem_limit_bytes=LIMIT),
        cost_estimate=pl.CostEstimate(flops=0, bytes_accessed=0, transcendentals=0),
    )(*in_hbm(keys, values, queries, steps))


def join_kernel(*refs):
    out = refs[-1]
    rows = 0
    for ref in refs[:-1]:
        height = ref.shape[1]
        out[:, rows : rows + height] = ref[...]
        rows += height


def join(parts):
    planes, _, width = parts[0].shape
    rows = sum(part.shape[1] for part in parts)
    return pl.pallas_call(
        join_kernel,
        in_specs=[VMEM] * len(parts),
        out_specs=VMEM,
        out_shape=jax.ShapeDtypeStruct((planes, rows, width), bf16),
        compiler_params=pltpu.CompilerParams(vmem_limit_bytes=LIMIT),
        cost_estimate=pl.CostEstimate(flops=0, bytes_accessed=0, transcendentals=0),
        name="join",
    )(*parts)


def step_rows(old, delta):
    previous = old.astype(f32)
    updated = previous + delta
    old_norm = jnp.sqrt(jnp.sum(previous * previous, axis=-1, keepdims=True) + epsilon)
    new_norm = jnp.sqrt(jnp.sum(updated * updated, axis=-1, keepdims=True) + epsilon)
    return (updated * (old_norm / new_norm)).astype(bf16)


def advance_rows(keys, target, gate, up, down):
    gate_pre = nt(gate, keys)
    up_pre = nt(up, keys)
    back_grad = nt(down, target)
    sig = sigmoid(gate_pre)
    silu = gate_pre * sig
    hidden = (silu * up_pre).astype(bf16)
    grad_up = (back_grad * silu).astype(bf16)
    grad_gate = ((back_grad * up_pre) * (sig * (1.0 + (gate_pre - silu)))).astype(bf16)
    return (
        step_rows(gate, nn(grad_gate, keys)),
        step_rows(up, nn(grad_up, keys)),
        step_rows(down, nn(hidden, target)),
    )


def serve_rows(queries, gate, up, down):
    c = nt(queries, gate)
    e = nt(queries, up)
    return nn((c * sigmoid(c) * e).astype(bf16), down)


def unit_kernel(tick, n_pieces, block, flags_ref, *refs):
    refs = list(refs)
    take = lambda n: [refs.pop(0) for _ in range(n)]
    tokens = take(4 if tick == 0 else 1)
    pieces = take(n_pieces)
    if tick == EXTRA:
        ans_out, new_ref, tok, acc, ans, sems = refs

        @pl.when(flags_ref[0] != 0)
        def _():
            unit_steps(
                tick, block, flags_ref, tokens, pieces, new_ref, new_ref, ans_out, tok,
                acc, ans, sems,
            )
    else:
        unit_steps(tick, block, flags_ref, tokens, pieces, *refs)


def unit_steps(
    tick, block, flags_ref, tokens, pieces, state, new_ref, ans_out, tok, acc, ans, sems
):
    if tick == 0:
        sources = [tokens[i].at[0, 0] for i in range(3)]
        state = state.at[0]
    else:
        sources = [tokens[0].at[i] for i in range(3)]
        state = new_ref
    loads = [pltpu.make_async_copy(sources[i], tok.at[i], sems.at[i]) for i in range(3)]
    for load in loads:
        load.start()
    if pieces:
        @pl.when(flags_ref[max(tick, 0)] != 0)
        def _():
            rows = 0
            copies = []
            for n, piece in enumerate(pieces):
                height = piece.shape[1]
                part = new_ref.at[:, pl.ds(rows, height)]
                copies.append(pltpu.make_async_copy(piece, part, sems.at[4 + n]))
                rows += height
            for copy in copies:
                copy.start()
            for copy in copies:
                copy.wait()

    loads[0].wait()
    loads[1].wait()
    if tick == 0:
        tok[1] = scaled_values(tokens[3][0, 0:1, :], tok[1])
    count = new_ref.shape[1] // block

    def one(rows, first, last):
        new = advance_rows(tok[0], tok[1], state[0, rows], state[1, rows], state[2, rows])
        for i in range(3):
            new_ref[i, rows] = new[i]
        if first:
            loads[2].wait()
        part = serve_rows(tok[2], new_ref[0, rows], new_ref[1, rows], new_ref[2, rows])
        total = part if first else acc[...] + part
        if last:
            ans[...] = total.astype(bf16)
        else:
            acc[...] = total

    if tick == EXTRA:
        loads[2].wait()
        acc[...] = jnp.zeros_like(acc)

        @pl.loop(0, count)
        def _(j):
            one(pl.ds(pl.multiple_of(j * block, block), block), False, False)

        ans[...] = acc[...].astype(bf16)
    else:
        for j in range(count):
            one(pl.ds(j * block, block), j == 0, j == count - 1)
    out = pltpu.make_async_copy(ans, ans_out.at[0, 0] if tick == 0 else ans_out, sems.at[3])
    out.start()
    out.wait()


def unit(tick, flags, tokens, state, pieces, block=512):
    span, width = tokens[0].shape[-2:]
    if tick == EXTRA:
        hid = sum(piece.shape[1] for piece in pieces)
        states, state_shapes = [], []
        aliases = {}
    else:
        hid = state.shape[-2]
        states = [state]
        state_shapes = [jax.ShapeDtypeStruct((3, hid, width), bf16)]
        aliases = {} if tick == 0 else {1 + len(tokens) + len(pieces): 0}
    rows = [pltpu.VMEM((3, hid, width), bf16)] if tick == EXTRA else []
    token_specs = [HBM] * len(tokens)
    if tick == 0:
        token_specs[3] = VMEM
        tokens = in_hbm(*tokens[:3]) + tokens[3:]
    return pl.pallas_call(
        functools.partial(unit_kernel, tick, len(pieces), block),
        in_specs=[SMEM] + token_specs + [HBM] * len(pieces) + [VMEM] * len(states),
        out_specs=[VMEM] * len(states) + [HBM],
        out_shape=state_shapes
        + [jax.ShapeDtypeStruct(tokens[0].shape if tick == 0 else (span, width), bf16)],
        input_output_aliases=aliases,
        scratch_shapes=rows
        + [
            pltpu.VMEM((3, span, width), bf16),
            pltpu.VMEM((span, width), f32),
            pltpu.VMEM((span, width), bf16),
            pltpu.SemaphoreType.DMA((4 + len(pieces),)),
        ],
        compiler_params=pltpu.CompilerParams(vmem_limit_bytes=LIMIT),
        cost_estimate=pl.CostEstimate(flops=0, bytes_accessed=0, transcendentals=0),
    )(flags, *tokens, *pieces, *states)


def body(fast_state, initial_fast, queries, token_keys, token_values, step_sizes):
    count = lax.axis_size("seq")
    position = lax.axis_index("seq")
    ticks = token_keys.shape[1]
    flags = jnp.stack(
        [(position == count - 1).astype(jnp.int32)]
        + [
            (position + t == count).astype(jnp.int32) for t in range(1, ticks - 1)
        ]
        + [(position + ticks > count + 1).astype(jnp.int32)]
    )

    def send(value, pairs):
        return lax.ppermute(value, "seq", pairs)

    def shift(value, steps):
        pairs = [(s, (s + steps) % count) for s in range(count)]
        if abs(steps) == ticks - 1:
            pairs = [p for p in pairs if set(p) != {0, count - steps if steps > 0 else count + steps}]
        return send(value, pairs)

    quads = count // 4
    cross = [(4 * q + c, 4 * q + c + 2) for q in range(quads) for c in (0, 1)]
    got = [send(initial_fast, cross)]
    held = initial_fast
    args = [token_keys, token_values, queries, step_sizes]
    packs = [pack(t, *args) for t in range(1, ticks)]
    tokens = [shift(packs[t - 1][0], -t) for t in range(1, ticks - 1)]
    whole_last, learn_last, ask_last = packs[-1]
    far = ticks - 1
    straight = [(s, s - far) for s in range(far, count)]
    learn_last = send(learn_last, straight)
    ask_last = send(ask_last, straight)
    wrapped = send(whole_last, [(s, s - far + count) for s in range(1, far)])
    tokens_x = send(whole_last, [(0, count - 1)])
    width = quads
    while width > 1:
        held = join([held] + got)
        radix = 4 if width % 4 == 0 else 2
        width //= radix
        base = quads - width
        got = [
            send(
                held,
                [
                    (4 * (base - j * width + i) + c, 4 * (base + i) + c)
                    for i in range(width)
                    for c in (2, 3)
                ],
            )
            for j in range(1, radix)
        ]
    held = join([held] + got)
    swapped = send(held, [(count - 2, count - 1), (count - 1, count - 2)])
    pieces = [held, swapped]

    state, out = unit(0, flags, args, fast_state, [])
    state, answer1 = unit(1, flags, tokens[:1], state, pieces)
    (answer_x,) = unit(EXTRA, flags, [tokens_x], None, in_hbm(*pieces))
    back = [shift(answer1, 1)]
    for t in range(2, ticks - 1):
        state, answer = unit(t, flags, tokens[t - 1 : t], state, pieces)
        if t == ticks - 2:
            state = keep(state)
        back.append(shift(answer, t))
    state = advance_only(far, flags, learn_last, wrapped, state)
    answer = serve_only(far, flags, ask_last, wrapped, state)
    back.append(shift(answer, far))
    back_x = send(answer_x, [(count - 1, 0)])
    back[-1] = jnp.where(position == 0, back_x, back[-1])
    for t in range(1, ticks):
        out = lax.dynamic_update_slice(out, back[t - 1][None, None], (0, t, 0, 0))
    return out


def pick(wrapped, usual, other):
    @pl.when(wrapped != 0)
    def _():
        for load in other:
            load.start()

    @pl.when(wrapped == 0)
    def _():
        for load in usual:
            load.start()


def advance_kernel(slot, block, flags_ref, tokens_ref, wrap_ref, state_ref, new_ref, tok, sems):
    del state_ref
    loads, other = [
        [pltpu.make_async_copy(ref.at[i], tok.at[i], sems.at[i]) for i in range(2)]
        for ref in (tokens_ref, wrap_ref)
    ]
    pick(flags_ref[slot], loads, other)
    for load in loads:
        load.wait()
    for j in range(new_ref.shape[1] // block):
        rows = pl.ds(j * block, block)
        new = advance_rows(
            tok[0], tok[1], new_ref[0, rows], new_ref[1, rows], new_ref[2, rows]
        )
        for i in range(3):
            new_ref[i, rows] = new[i]


def advance_only(slot, flags, tokens, wrapped, state, block=512):
    return pl.pallas_call(
        functools.partial(advance_kernel, slot, block),
        in_specs=[SMEM, HBM, HBM, VMEM],
        out_specs=VMEM,
        out_shape=jax.ShapeDtypeStruct(state.shape, bf16),
        input_output_aliases={3: 0},
        scratch_shapes=[pltpu.VMEM(tokens.shape, bf16), pltpu.SemaphoreType.DMA((2,))],
        compiler_params=pltpu.CompilerParams(vmem_limit_bytes=LIMIT),
        cost_estimate=pl.CostEstimate(flops=0, bytes_accessed=0, transcendentals=0),
        name="advance",
    )(flags, tokens, wrapped, state)


def serve_kernel(
    slot, block, flags_ref, queries_ref, wrap_ref, state_ref, ans_ref, asked, acc, sem
):
    load = pltpu.make_async_copy(queries_ref, asked, sem)
    other = pltpu.make_async_copy(wrap_ref.at[2], asked, sem)
    pick(flags_ref[slot], [load], [other])
    load.wait()
    count = state_ref.shape[1] // block
    for j in range(count):
        rows = pl.ds(j * block, block)
        part = serve_rows(
            asked[...], state_ref[0, rows], state_ref[1, rows], state_ref[2, rows]
        )
        total = part if j == 0 else acc[...] + part
        if j == count - 1:
            ans_ref[...] = total.astype(bf16)
        else:
            acc[...] = total


def serve_only(slot, flags, queries, wrapped, state, block=512):
    return pl.pallas_call(
        functools.partial(serve_kernel, slot, block),
        in_specs=[SMEM, HBM, HBM, VMEM],
        out_specs=VMEM,
        out_shape=jax.ShapeDtypeStruct(queries.shape, bf16),
        scratch_shapes=[
            pltpu.VMEM(queries.shape, bf16),
            pltpu.VMEM(queries.shape, f32),
            pltpu.SemaphoreType.DMA,
        ],
        compiler_params=pltpu.CompilerParams(vmem_limit_bytes=LIMIT),
        cost_estimate=pl.CostEstimate(flops=0, bytes_accessed=0, transcendentals=0),
        name="serve",
    )(flags, queries, wrapped, state)


def keep_kernel(state_ref, kept_ref):
    del state_ref, kept_ref


def keep(state):
    return pl.pallas_call(
        keep_kernel,
        in_specs=[VMEM],
        out_specs=VMEM,
        out_shape=jax.ShapeDtypeStruct(state.shape, state.dtype),
        input_output_aliases={0: 0},
        cost_estimate=pl.CostEstimate(flops=0, bytes_accessed=0, transcendentals=0),
        compiler_params=pltpu.CompilerParams(vmem_limit_bytes=1 << 20),
        name="keep",
    )(state)


def solution(mesh):
    return jax.shard_map(
        body,
        mesh=mesh,
        in_specs=(
            P(("grp", "seq"), None, None, None),
            P(None, "seq", None),
            P(("grp", "seq"), None, None, None),
            P(("grp", "seq"), None, None, None),
            P(("grp", "seq"), None, None, None),
            P(("grp", "seq"), None, None),
        ),
        out_specs=P(("grp", "seq"), None, None, None),
        check_vma=False,
    )
```

```python
import functools
import jax
import jax.numpy as jnp
from jax import lax
from jax.experimental import pallas as pl
from jax.experimental.pallas import tpu as pltpu
from jax.sharding import PartitionSpec as P

epsilon = 1e-06
f32 = jnp.float32
bf16 = jnp.bfloat16
HBM = pl.BlockSpec(memory_space=pltpu.HBM)
VMEM = pl.BlockSpec(memory_space=pltpu.VMEM)
SMEM = pl.BlockSpec(memory_space=pltpu.SMEM)
LIMIT = 28 << 20
EXTRA = -1


def in_hbm(*arrays):
    return [pltpu.with_memory_space_constraint(a, pltpu.HBM) for a in arrays]


def nt(a, b):
    return lax.dot_general(a, b, (((1,), (1,)), ((), ())), preferred_element_type=f32)


def nn(a, b):
    return lax.dot_general(a, b, (((1,), (0,)), ((), ())), preferred_element_type=f32)


def sigmoid(x):
    return 0.5 * jnp.tanh(0.5 * x) + 0.5


def scaled_values(steps_row, values):
    lanes = 128
    span, width = values.shape
    column = jnp.broadcast_to(steps_row.astype(f32), (lanes, span)).T
    return jnp.concatenate(
        [
            (column * values[:, i : i + lanes].astype(f32)).astype(bf16)
            for i in range(0, width, lanes)
        ],
        axis=1,
    )


def pack_kernel(tick, split, k_ref, v_ref, q_ref, r_hbm, *refs):
    o_ref = refs[0]
    tok, r_ref, sems = refs[-3:]
    rates = pltpu.make_async_copy(r_hbm, r_ref, sems.at[6])
    rates.start()
    sources = (k_ref, v_ref, q_ref)
    loads = [
        pltpu.make_async_copy(sources[i].at[0, tick], tok.at[i], sems.at[i])
        for i in range(3)
    ]
    stores = [
        [pltpu.make_async_copy(tok.at[i], o_ref.at[i], sems.at[3 + i])] for i in range(3)
    ]
    if split:
        parts = (refs[1].at[0], refs[1].at[1], refs[2])
        for i in range(3):
            stores[i].append(pltpu.make_async_copy(tok.at[i], parts[i], sems.at[7 + i]))
    for i in (1, 0, 2):
        loads[i].start()
    rates.wait()
    loads[1].wait()
    tok[1] = scaled_values(r_ref[0, tick : tick + 1, :], tok[1])
    for i in (1, 0, 2):
        if i != 1:
            loads[i].wait()
        for store in reversed(stores[i]):
            store.start()
    for group in stores:
        for store in group:
            store.wait()


def pack(tick, keys, values, queries, steps):
    _, ticks, span, width = keys.shape
    split = tick == ticks - 1
    shapes = [(3, span, width)]
    if split:
        shapes += [(2, span, width), (span, width)]
    return pl.pallas_call(
        functools.partial(pack_kernel, tick, split),
        in_specs=[HBM] * 4,
        out_specs=[HBM] * len(shapes),
        out_shape=[jax.ShapeDtypeStruct(shape, bf16) for shape in shapes],
        scratch_shapes=[
            pltpu.VMEM((3, span, width), bf16),
            pltpu.VMEM(steps.shape, bf16),
            pltpu.SemaphoreType.DMA((10,)),
        ],
        compiler_params=pltpu.CompilerParams(vmem_limit_bytes=LIMIT),
        cost_estimate=pl.CostEstimate(flops=0, bytes_accessed=0, transcendentals=0),
    )(*in_hbm(keys, values, queries, steps))


def join_kernel(*refs):
    out = refs[-1]
    rows = 0
    for ref in refs[:-1]:
        height = ref.shape[1]
        out[:, rows : rows + height] = ref[...]
        rows += height


def join(parts):
    planes, _, width = parts[0].shape
    rows = sum(part.shape[1] for part in parts)
    return pl.pallas_call(
        join_kernel,
        in_specs=[VMEM] * len(parts),
        out_specs=VMEM,
        out_shape=jax.ShapeDtypeStruct((planes, rows, width), bf16),
        compiler_params=pltpu.CompilerParams(vmem_limit_bytes=LIMIT),
        cost_estimate=pl.CostEstimate(flops=0, bytes_accessed=0, transcendentals=0),
        name="join",
    )(*parts)


def step_rows(old, delta):
    previous = old.astype(f32)
    updated = previous + delta
    old_norm = jnp.sqrt(jnp.sum(previous * previous, axis=-1, keepdims=True) + epsilon)
    new_norm = jnp.sqrt(jnp.sum(updated * updated, axis=-1, keepdims=True) + epsilon)
    return (updated * (old_norm / new_norm)).astype(bf16)


def advance_rows(keys, target, gate, up, down):
    gate_pre = nt(gate, keys)
    up_pre = nt(up, keys)
    back_grad = nt(down, target)
    sig = sigmoid(gate_pre)
    silu = gate_pre * sig
    hidden = (silu * up_pre).astype(bf16)
    grad_up = (back_grad * silu).astype(bf16)
    grad_gate = ((back_grad * up_pre) * (sig * (1.0 + (gate_pre - silu)))).astype(bf16)
    return (
        step_rows(gate, nn(grad_gate, keys)),
        step_rows(up, nn(grad_up, keys)),
        step_rows(down, nn(hidden, target)),
    )


def serve_rows(queries, gate, up, down):
    c = nt(queries, gate)
    e = nt(queries, up)
    return nn((c * sigmoid(c) * e).astype(bf16), down)


def unit_kernel(tick, n_pieces, block, flags_ref, *refs):
    refs = list(refs)
    take = lambda n: [refs.pop(0) for _ in range(n)]
    tokens = take(4 if tick == 0 else 1)
    pieces = take(n_pieces)
    if tick == EXTRA:
        ans_out, new_ref, tok, acc, _, sems = refs

        @pl.when(flags_ref[0] != 0)
        def _():
            unit_steps(
                tick, block, flags_ref, tokens, pieces, new_ref, new_ref, ans_out, tok,
                acc, ans_out, sems,
            )
    else:
        unit_steps(tick, block, flags_ref, tokens, pieces, *refs)


def unit_steps(
    tick, block, flags_ref, tokens, pieces, state, new_ref, ans_out, tok, acc, ans, sems
):
    if tick == 0:
        sources = [tokens[i].at[0, 0] for i in range(3)]
        state = state.at[0]
    else:
        sources = [tokens[0].at[i] for i in range(3)]
        state = new_ref
    loads = [pltpu.make_async_copy(sources[i], tok.at[i], sems.at[i]) for i in range(3)]
    for load in loads:
        load.start()
    brought = []
    if pieces:
        rows = 0
        for n, piece in enumerate(pieces):
            height = piece.shape[1]
            part = new_ref.at[:, pl.ds(rows, height)]
            copy = pltpu.make_async_copy(piece, part, sems.at[4 + n])
            brought.append((rows // block, copy))
            rows += height

        @pl.when(flags_ref[max(tick, 0)] != 0)
        def _():
            for _, copy in brought:
                copy.start()

    loads[0].wait()
    loads[1].wait()
    if tick == 0:
        tok[1] = scaled_values(tokens[3][0, 0:1, :], tok[1])
    count = new_ref.shape[1] // block

    for j in range(count):
        rows = pl.ds(j * block, block)
        due = [copy for at, copy in brought if at == j]
        if due:
            @pl.when(flags_ref[max(tick, 0)] != 0)
            def _():
                for copy in due:
                    copy.wait()

        new = advance_rows(tok[0], tok[1], state[0, rows], state[1, rows], state[2, rows])
        for i in range(3):
            new_ref[i, rows] = new[i]
        if j == 0:
            loads[2].wait()
        part = serve_rows(tok[2], new_ref[0, rows], new_ref[1, rows], new_ref[2, rows])
        total = part if j == 0 else acc[...] + part
        if j == count - 1:
            ans[...] = total.astype(bf16)
        else:
            acc[...] = total
    if tick == EXTRA:
        return
    out = pltpu.make_async_copy(ans, ans_out.at[0, 0] if tick == 0 else ans_out, sems.at[3])
    out.start()
    out.wait()


def unit(tick, flags, tokens, state, pieces, block=512):
    span, width = tokens[0].shape[-2:]
    if tick == EXTRA:
        hid = sum(piece.shape[1] for piece in pieces)
        states, state_shapes = [], []
        aliases = {}
    else:
        hid = state.shape[-2]
        states = [state]
        state_shapes = [jax.ShapeDtypeStruct((3, hid, width), bf16)]
        aliases = {} if tick == 0 else {1 + len(tokens) + len(pieces): 0}
    rows = [pltpu.VMEM((3, hid, width), bf16)] if tick == EXTRA else []
    token_specs = [HBM] * len(tokens)
    if tick == 0:
        token_specs[3] = VMEM
        tokens = in_hbm(*tokens[:3]) + tokens[3:]
    return pl.pallas_call(
        functools.partial(unit_kernel, tick, len(pieces), block),
        in_specs=[SMEM] + token_specs + [HBM] * len(pieces) + [VMEM] * len(states),
        out_specs=[VMEM] * len(states) + [VMEM if tick == EXTRA else HBM],
        out_shape=state_shapes
        + [jax.ShapeDtypeStruct(tokens[0].shape if tick == 0 else (span, width), bf16)],
        input_output_aliases=aliases,
        scratch_shapes=rows
        + [
            pltpu.VMEM((3, span, width), bf16),
            pltpu.VMEM((span, width), f32),
            pltpu.VMEM((span, width), bf16),
            pltpu.SemaphoreType.DMA((4 + len(pieces),)),
        ],
        compiler_params=pltpu.CompilerParams(vmem_limit_bytes=LIMIT),
        cost_estimate=pl.CostEstimate(flops=0, bytes_accessed=0, transcendentals=0),
    )(flags, *tokens, *pieces, *states)


def body(fast_state, initial_fast, queries, token_keys, token_values, step_sizes):
    count = lax.axis_size("seq")
    position = lax.axis_index("seq")
    ticks = token_keys.shape[1]
    flags = jnp.stack(
        [(position == count - 1).astype(jnp.int32)]
        + [
            ((position + t == count) & (t < ticks - 1)).astype(jnp.int32)
            for t in range(1, ticks)
        ]
    )

    def send(value, pairs):
        return lax.ppermute(value, "seq", pairs)

    def shift(value, steps):
        pairs = [(s, (s + steps) % count) for s in range(count)]
        if abs(steps) == ticks - 1:
            pairs = [p for p in pairs if set(p) != {0, count - steps if steps > 0 else count + steps}]
        return send(value, pairs)

    quads = count // 4
    cross = [(4 * q + c, 4 * q + c + 2) for q in range(quads) for c in (0, 1)]
    got = [send(initial_fast, cross)]
    held = initial_fast
    args = [token_keys, token_values, queries, step_sizes]
    packs = [pack(t, *args) for t in range(1, ticks)]
    tokens = [shift(packs[t - 1][0], -t) for t in range(1, ticks - 1)]
    whole_last, learn_last, ask_last = packs[-1]
    learn_last = shift(learn_last, 1 - ticks)
    ask_last = shift(ask_last, 1 - ticks)
    tokens_x = send(whole_last, [(0, count - 1)])
    width = quads
    while width > 1:
        held = join([held] + got)
        radix = 4 if width % 4 == 0 else 2
        width //= radix
        base = quads - width
        got = [
            send(
                held,
                [
                    (4 * (base - j * width + i) + c, 4 * (base + i) + c)
                    for i in range(width)
                    for c in (2, 3)
                ],
            )
            for j in range(1, radix)
        ]
    held = join([held] + got)
    swapped = send(held, [(count - 2, count - 1), (count - 1, count - 2)])
    pieces = [held, swapped]

    state, out = unit(0, flags, args, fast_state, [])
    state, answer1 = unit(1, flags, tokens[:1], state, pieces)
    (answer_x,) = unit(EXTRA, flags, [tokens_x], None, in_hbm(*pieces))
    back = [shift(answer1, 1)]
    for t in range(2, ticks - 1):
        state, answer = unit(t, flags, tokens[t - 1 : t], state, pieces)
        if t == ticks - 2:
            state = keep(state)
        back.append(shift(answer, t))
    state = advance_only(learn_last, state)
    back.append(shift(serve_only(ask_last, state), ticks - 1))
    back_x = send(answer_x, [(count - 1, 0)])
    back[-1] = jnp.where(position == 0, back_x, back[-1])
    for t in range(1, ticks):
        out = lax.dynamic_update_slice(out, back[t - 1][None, None], (0, t, 0, 0))
    return out


def advance_kernel(block, tokens_ref, state_ref, new_ref, tok, sems):
    del state_ref
    loads = [
        pltpu.make_async_copy(tokens_ref.at[i], tok.at[i], sems.at[i]) for i in range(2)
    ]
    for load in loads:
        load.start()
    for load in loads:
        load.wait()
    for j in range(new_ref.shape[1] // block):
        rows = pl.ds(j * block, block)
        new = advance_rows(
            tok[0], tok[1], new_ref[0, rows], new_ref[1, rows], new_ref[2, rows]
        )
        for i in range(3):
            new_ref[i, rows] = new[i]


def advance_only(tokens, state, block=512):
    return pl.pallas_call(
        functools.partial(advance_kernel, block),
        in_specs=[HBM, VMEM],
        out_specs=VMEM,
        out_shape=jax.ShapeDtypeStruct(state.shape, bf16),
        input_output_aliases={1: 0},
        scratch_shapes=[pltpu.VMEM(tokens.shape, bf16), pltpu.SemaphoreType.DMA((2,))],
        compiler_params=pltpu.CompilerParams(vmem_limit_bytes=LIMIT),
        cost_estimate=pl.CostEstimate(flops=0, bytes_accessed=0, transcendentals=0),
        name="advance",
    )(tokens, state)


def serve_kernel(block, queries_ref, state_ref, ans_ref, asked, acc, sem):
    load = pltpu.make_async_copy(queries_ref, asked, sem)
    load.start()
    load.wait()
    count = state_ref.shape[1] // block
    for j in range(count):
        rows = pl.ds(j * block, block)
        part = serve_rows(
            asked[...], state_ref[0, rows], state_ref[1, rows], state_ref[2, rows]
        )
        total = part if j == 0 else acc[...] + part
        if j == count - 1:
            ans_ref[...] = total.astype(bf16)
        else:
            acc[...] = total


def serve_only(queries, state, block=512):
    return pl.pallas_call(
        functools.partial(serve_kernel, block),
        in_specs=[HBM, VMEM],
        out_specs=VMEM,
        out_shape=jax.ShapeDtypeStruct(queries.shape, bf16),
        scratch_shapes=[
            pltpu.VMEM(queries.shape, bf16),
            pltpu.VMEM(queries.shape, f32),
            pltpu.SemaphoreType.DMA,
        ],
        compiler_params=pltpu.CompilerParams(vmem_limit_bytes=LIMIT),
        cost_estimate=pl.CostEstimate(flops=0, bytes_accessed=0, transcendentals=0),
        name="serve",
    )(queries, state)


def keep_kernel(state_ref, kept_ref):
    del state_ref, kept_ref


def keep(state):
    return pl.pallas_call(
        keep_kernel,
        in_specs=[VMEM],
        out_specs=VMEM,
        out_shape=jax.ShapeDtypeStruct(state.shape, state.dtype),
        input_output_aliases={0: 0},
        cost_estimate=pl.CostEstimate(flops=0, bytes_accessed=0, transcendentals=0),
        compiler_params=pltpu.CompilerParams(vmem_limit_bytes=1 << 20),
        name="keep",
    )(state)


def solution(mesh):
    return jax.shard_map(
        body,
        mesh=mesh,
        in_specs=(
            P(("grp", "seq"), None, None, None),
            P(None, "seq", None),
            P(("grp", "seq"), None, None, None),
            P(("grp", "seq"), None, None, None),
            P(("grp", "seq"), None, None, None),
            P(("grp", "seq"), None, None),
        ),
        out_specs=P(("grp", "seq"), None, None, None),
        check_vma=False,
    )
```
